256 devices in a mesh: row: 8 (over y, core), col: 32 (over x, z).
Axes of the slice: x: 4, y: 4, z: 8, core: 2. Of those that a mesh axis runs over, the one named last changes fastest.
Arguments:
- stored: float32 [20, 8, 128, 5, 32, 128], P(None, 'row', None, None, 'col'), may hold values from -1 to 13, as said below
- rhs: float32 [5, 32, 128, 128], P(None, 'col'), may hold values from -60 to 60
Outputs:
- solution: float32 [5, 32, 128, 128], P(None, 'col')
- residual: float32 [5, 32, 128, 128], P(None, 'col')
The draws below stay inside these ranges and needn't reach their ends.
Inputs may be any that keep to these rules, and one draw needn't show every extreme that they name: `stored`: the operator A built from it as in the reference program is symmetric positive definite.
All inputs are finite; a program needn't handle non-finite values.
Results may differ from the reference program's by a relative error of at most 0.0003.
Values sent between devices are 32-bit elements; how exact they have to be, the bound alone decides.
A program may use at most 128 MiB of HBM per device.

```python
import math
import jax
import jax.numpy as jnp
from jax import lax

NORD = 20480
BS = 128
K = 128
ITERS = 2
NB = 160
LR = 20
LC = 5


def draw_stored(key, part):
    noise_key, diag_key = jax.random.split(key, 2)
    entries = jax.random.truncated_normal(noise_key, -6.0, 6.0, (NORD, NORD), jnp.float32)
    entries = entries / math.sqrt(NORD)
    diagonal = jax.random.uniform(diag_key, (NORD,), jnp.float32, 3.0, 5.0)
    flattened = entries.reshape(-1).at[jnp.arange(NORD, dtype=jnp.int32) * (NORD + 1)].set(diagonal)
    matrix = flattened.reshape(NORD, NORD)
    return matrix.reshape(LR, NB // LR, BS, LC, NB // LC, BS)


def draw_rhs(key, part):
    base_key, row_key, col_key = jax.random.split(key, 3)
    row_scale = jnp.exp(jax.random.uniform(row_key, (NORD,), jnp.float32, math.log(0.3), math.log(3.0)))
    col_scale = jnp.exp(jax.random.uniform(col_key, (K,), jnp.float32, math.log(0.3), math.log(3.0)))
    values = jax.random.truncated_normal(base_key, -4.0, 4.0, (NORD, K), jnp.float32)
    values = values * row_scale[:, None] * col_scale[None, :]
    return values.reshape(LC, NB // LC, BS, K)


def setup_inputs(seed: int = 0) -> dict:
    splits = jax.random.split(jax.random.key(seed), 3)
    stored = draw_stored(jax.random.fold_in(splits[2], 71), 0)
    rhs = draw_rhs(jax.random.fold_in(splits[2], 71), 0)
    return dict(stored=stored, rhs=rhs)


HIGHEST = lax.Precision.HIGHEST

def gram_local(left_side, right_side):
    return jnp.dot(left_side.T.astype(jnp.float32), right_side.astype(jnp.float32), precision=HIGHEST, preferred_element_type=jnp.float32)

def mix_right(vectors, matrix):
    return jnp.dot(vectors.astype(jnp.float32), matrix.astype(jnp.float32), precision=HIGHEST, preferred_element_type=jnp.float32)

def solve_spd(matrix, target):
    factor = jnp.linalg.cholesky(matrix)
    return jax.scipy.linalg.cho_solve((factor, True), target)

def reference(stored, rhs):
    block_count = NORD // BS
    blocks = stored.reshape(block_count, BS, block_count, BS)
    indices = jnp.arange(block_count, dtype=jnp.int32)
    weight = jnp.where(indices[:, None] > indices[None, :], 1.0, jnp.where(indices[:, None] == indices[None, :], 0.5, 0.0)).astype(jnp.float32)
    lower_part = (blocks * weight[:, None, :, None]).reshape(NORD, NORD)
    operator = lower_part + lower_part.T
    right_side = rhs.reshape(NORD, K)
    solution = jnp.zeros_like(right_side)
    residual = right_side
    direction = right_side
    gram_now = gram_local(residual, residual)
    for iteration in range(ITERS):
        applied = jnp.dot(operator.astype(jnp.float32), direction.astype(jnp.float32), precision=HIGHEST, preferred_element_type=jnp.float32)
        curvature = gram_local(direction, applied)
        step_size = solve_spd(curvature, gram_now)
        solution = solution + mix_right(direction, step_size)
        residual = residual - mix_right(applied, step_size)
        if iteration + 1 < ITERS:
            gram_next = gram_local(residual, residual)
            mix_factor = solve_spd(gram_now, gram_next)
            direction = residual + mix_right(direction, mix_factor)
            gram_now = gram_next
    return (solution.reshape(rhs.shape), residual.reshape(rhs.shape))
```

```python
import functools

import jax
import jax.numpy as jnp
from jax import lax
from jax.experimental import pallas as pl
from jax.experimental.pallas import tpu as pltpu
from jax.sharding import PartitionSpec as P

MESH = pl.DeviceIdType.MESH
HIGHEST = lax.Precision.HIGHEST
F32 = jnp.float32
BF16 = jnp.bfloat16

ROWS = 8
XS = 4
ZS = 8
NBC = 5
BS = 128
K = 128
SET = NBC * BS
PART = SET // ROWS
GP = K // ROWS


def dot(a, b):
    return jnp.dot(a, b, precision=HIGHEST, preferred_element_type=F32)


def dot_t(a, b):
    return lax.dot_general(
        a, b, (((0,), (0,)), ((), ())), precision=HIGHEST, preferred_element_type=F32
    )


def halves(value):
    high = value.astype(BF16)
    low = (value - high.astype(F32)).astype(BF16)
    return high, low


def kernel(
    stored, rhs, out_x, out_r,
    araw, ahi, alo, cb, cw, cv, chl, rb, rw, rt, yt,
    p, rx, q, rz, yv, ry, own,
    gsrc, grs, gfull, gz, gx, mat,
    ld_sem, snd, snd0, rb_z, rb_x, x_sem, z_sem, y_sem, c_sem, rw_z, rw_x,
    grs_sem, gag_sem, gz_sem, gx_sem,
):
    r = lax.axis_index("row")
    c = lax.axis_index("col")
    x = c // ZS
    z = lax.rem(c, ZS)
    diagonal = r == z

    def send(src, dst, ssem, rsem, row, xx, zz):
        pltpu.make_async_remote_copy(
            src_ref=src, dst_ref=dst, send_sem=ssem, recv_sem=rsem,
            device_id=(row, xx * ZS + zz), device_id_type=MESH,
        ).start()

    def await_bytes(ref, sem):
        pltpu.make_async_copy(ref, ref, sem).wait()

    def await_sent(sem, rows):
        part = araw.at[pl.ds(0, rows)]
        pltpu.make_async_copy(part, part, sem).wait()

    load_b = pltpu.make_async_copy(rhs, cb, ld_sem.at[NBC])
    load_b.start()
    span = XS * SET

    def load_a(b):
        rows = pl.ds(b * span, span)
        return pltpu.make_async_copy(stored.at[rows], araw.at[rows], ld_sem.at[b])

    for b in range(NBC):
        load_a(b).start()

    barrier = pltpu.get_barrier_semaphore()

    def greet(row, xx, zz):
        pl.semaphore_signal(barrier, inc=1, device_id=(row, xx * ZS + zz), device_id_type=MESH)

    @pl.loop(1, 8)
    def _(k):
        greet(r, x, lax.rem(z + k, ZS))
        greet(lax.rem(r + k, ROWS), x, z)
        greet(z, x, lax.rem(z + k, ZS))
        greet(lax.rem(r + k, ROWS), x, r)

    @pl.loop(1, XS)
    def _(k):
        greet(r, lax.rem(x + k, XS), z)

    @pl.when(jnp.logical_not(diagonal))
    def _():
        greet(z, x, z)
        greet(r, x, r)
        pl.semaphore_wait(barrier, 33)

    @pl.when(diagonal)
    def _():
        pl.semaphore_wait(barrier, 31)

    load_b.wait()

    def to_z(dst_of, sem, rsem):

        @pl.loop(1, ZS)
        def _(k):
            t = lax.rem(z + k, ZS)
            s_ref, d_ref = dst_of(t)
            send(s_ref, d_ref, sem, rsem.at[z], r, x, t)

    def to_x(dst_of, sem, rsem):
        @pl.loop(1, XS)
        def _(k):
            t = lax.rem(x + k, XS)
            s_ref, d_ref = dst_of(t)
            send(s_ref, d_ref, sem, rsem.at[x], r, t, z)

    def to_r(dst_of, sem, rsem):
        @pl.loop(1, ROWS)
        def _(k):
            t = lax.rem(r + k, ROWS)
            s_ref, d_ref = dst_of(t)
            send(s_ref, d_ref, sem, rsem.at[r], t, x, z)

    def with_own(first, rest, src, dst, ssem0, rsem):
        @pl.when(diagonal)
        def _():
            pltpu.make_async_copy(src, dst, rsem).start()

        @pl.when(jnp.logical_not(diagonal))
        def _():
            send(src, dst, ssem0, rsem, *first)

        rest()

    def to_cross(src_of, dst, ssem, ssem0, rsem):
        def rest():
            @pl.loop(1, ZS)
            def _(k):
                t = lax.rem(z + k, ZS)
                send(src_of(t), dst, ssem, rsem.at[r], z, x, t)

        with_own((z, x, z), rest, src_of(z), dst, ssem0, rsem.at[r])

    def to_column(src, dst, ssem, ssem0, rsem):
        def rest():
            @pl.loop(1, ROWS)
            def _(k):
                t = lax.rem(r + k, ROWS)
                send(src, dst, ssem, rsem.at[z], t, x, r)

        with_own((r, x, r), rest, src, dst, ssem0, rsem.at[z])

    def part_rows(j):
        return pl.ds(pl.multiple_of(j * PART, 8), PART)

    def small_rows(j):
        return pl.ds(pl.multiple_of(j * GP, 8), GP)

    def split_columns(source):
        high, low = halves(source[...])
        chl[:, :K] = high
        chl[:, K:] = low

    def products_by_rows(m):
        for b in range(NBC):
            depth = (b + 1) * BS
            right = chl[:depth, :]
            both = jnp.dot(ahi[b, :, :depth], right, preferred_element_type=F32) + jnp.dot(
                alo[b, :, :depth], right, preferred_element_type=F32
            )
            total = both[:, :K] + both[:, K:]
            for xx in range(XS):
                p[m, xx, b * BS : (b + 1) * BS, :] = total[xx * BS : (xx + 1) * BS, :]

    def turn_rows(source):
        for b in range(NBC):

            @pl.loop(0, XS)
            def _(xx):
                high, low = halves(source[xx, b * BS : (b + 1) * BS, :].T)
                at = pl.ds(pl.multiple_of(xx * BS, BS), BS)
                rt[b, :K, at] = high
                rt[b, K:, at] = low

    def products_by_columns(m):
        for b in reversed(range(NBC)):
            depth = (b + 1) * BS
            left = rt[b]
            both = jnp.dot(left, ahi[b, :, :depth], preferred_element_type=F32) + jnp.dot(
                left, alo[b, :, :depth], preferred_element_type=F32
            )
            total = both[:K, :] + both[K:, :]
            if b == NBC - 1:
                yt[...] = total
            else:
                yt[:, :depth] += total
        for b in range(NBC):
            yv[m, b * BS : (b + 1) * BS, :] = yt[:, b * BS : (b + 1) * BS].T

    def gram_rows(left, right):
        def step(xx, total):
            return total + dot_t(left[xx], right[xx])

        return lax.fori_loop(0, XS, step, jnp.zeros((K, K), F32))

    def invert(source):
        mat[...] = source
        lanes = lax.broadcasted_iota(jnp.int32, (K, K), 1)
        subs = lax.broadcasted_iota(jnp.int32, (K, K), 0)
        lane_row = lax.broadcasted_iota(jnp.int32, (1, K), 1)

        @pl.loop(0, K)
        def _(j):
            row = mat[pl.ds(j, 1), :]
            now = mat[...]
            in_col = lanes == j
            col = jnp.sum(jnp.where(in_col, now, 0.0), axis=1, keepdims=True)
            pivot = jnp.sum(jnp.where(lane_row == j, row, 0.0), axis=1, keepdims=True)
            scaled = jnp.where(lane_row == j, 1.0, row) / pivot
            mat[...] = jnp.where(subs == j, scaled, jnp.where(in_col, 0.0, now) - col * scaled)

        return mat[...]

    def sum_start(k, value, sem):
        gsrc[k] = value
        to_r(lambda t: (gsrc.at[k, small_rows(t)], grs.at[k, r]), sem, grs_sem.at[k])

    def sum_middle(k):
        grs[k, r] = gsrc[k, small_rows(r)]

        @pl.loop(1, ROWS)
        def _(j):
            t = lax.rem(r + j, ROWS)
            await_bytes(grs.at[k, t], grs_sem.at[k, t])

        total = grs[k, 0]
        for j in range(1, ROWS):
            total = total + grs[k, j]
        return total

    def sum_spread(k, total, sem):
        gfull[k, small_rows(r)] = total
        piece = gfull.at[k, small_rows(r)]
        to_r(lambda t: (piece, piece), sem, gag_sem.at[k])

    def sum_end(k):
        @pl.loop(1, ROWS)
        def _(j):
            t = lax.rem(r + j, ROWS)
            await_bytes(gfull.at[k, small_rows(t)], gag_sem.at[k, t])

        return gfull[k]

    to_cross(
        lambda t: cb.at[part_rows(r)], rb.at[x, part_rows(r)], snd.at[0], snd0.at[0], rb_z
    )
    split_columns(cb)

    mine = x * ZS + z
    for b in range(NBC):
        load_a(b).wait()

        @pl.loop(0, XS)
        def _(xx):
            there = xx * ZS + r
            weight = jnp.where(there > mine, 1.0, jnp.where(there == mine, 0.5, 0.0)).astype(F32)
            at = pl.ds(pl.multiple_of(xx * BS, BS), BS)
            for bb in range(b + 1):
                block = araw[pl.ds((b * XS + xx) * SET + bb, BS, NBC), :]
                if bb == b:
                    block = block * weight
                high, low = halves(block)
                ahi[b, at, bb * BS : (bb + 1) * BS] = high
                alo[b, at, bb * BS : (bb + 1) * BS] = low

    def scatter_rows(m):
        to_x(lambda t: (p.at[m, t], rx.at[m, x]), snd.at[1 + m], x_sem.at[m])

    def scatter_rows_next(m):
        @pl.loop(1, XS)
        def _(k):
            t = lax.rem(x + k, XS)
            await_bytes(rx.at[m, t], x_sem.at[m, t])

        rx[m, x] = p[m, x]
        q[m] = (rx[m, 0] + rx[m, 1]) + (rx[m, 2] + rx[m, 3])
        to_z(lambda t: (q.at[m, part_rows(t)], rz.at[m, z]), snd.at[3 + m], z_sem.at[m])

    def scatter_columns(m):
        to_cross(
            lambda t: yv.at[m, part_rows(t)], ry.at[m, r], snd.at[5 + m], snd0.at[1 + m], y_sem.at[m]
        )

    def owned(m):
        rz[m, z] = q[m, part_rows(z)]

        @pl.loop(1, ZS)
        def _(k):
            t = lax.rem(z + k, ZS)
            await_bytes(rz.at[m, t], z_sem.at[m, t])

        @pl.loop(0, ROWS)
        def _(k):
            await_bytes(ry.at[m, k], y_sem.at[m, k])

        total = rz[m, 0] + ry[m, 0]
        for j in range(1, 8):
            total = total + (rz[m, j] + ry[m, j])
        own[m] = total

    def gather_columns(m, dst):
        to_column(
            own.at[m], dst.at[part_rows(z)], snd.at[7 + m], snd0.at[3 + m], c_sem.at[m]
        )

    def columns_here(m, dst):
        @pl.loop(0, ZS)
        def _(k):
            await_bytes(dst.at[part_rows(k)], c_sem.at[m, k])

    products_by_rows(0)
    scatter_rows(0)

    @pl.loop(0, ROWS)
    def _(k):
        await_bytes(rb.at[x, part_rows(k)], rb_z.at[k])

    to_x(lambda t: (rb.at[x], rb.at[x]), snd.at[9], rb_x)

    @pl.loop(1, XS)
    def _(k):
        t = lax.rem(x + k, XS)
        await_bytes(rb.at[t], rb_x.at[t])

    turn_rows(rb)
    products_by_columns(0)
    scatter_columns(0)
    sum_start(0, gram_rows(rb, rb), snd.at[10])
    scatter_rows_next(0)
    sum_spread(0, sum_middle(0), snd.at[11])
    gram0 = sum_end(0)
    gram0_inverse = invert(gram0)
    gsrc[4] = gram0_inverse
    owned(0)

    gather_columns(0, cw)
    rw[x, part_rows(z)] = own[0]
    to_z(lambda t: (own.at[0], rw.at[x, part_rows(z)]), snd.at[12], rw_z)
    columns_here(0, cw)
    split_columns(cw)
    products_by_rows(1)

    @pl.loop(1, ZS)
    def _(k):
        t = lax.rem(z + k, ZS)
        await_bytes(rw.at[x, part_rows(t)], rw_z.at[t])

    to_x(lambda t: (rw.at[x], rw.at[x]), snd.at[13], rw_x)
    scatter_rows(1)

    @pl.loop(1, XS)
    def _(k):
        t = lax.rem(x + k, XS)
        await_bytes(rw.at[t], rw_x.at[t])

    sum_start(1, gram_rows(rb, rw), snd.at[14])
    turn_rows(rw)
    products_by_columns(1)
    scatter_columns(1)
    scatter_rows_next(1)
    sum_spread(1, sum_middle(1), snd.at[15])
    curvature = sum_end(1)
    step = dot(invert(curvature), gfull[0])

    def residual_gram(xx, total):
        part = rb[xx] - dot(rw[xx], step)
        return total + dot_t(part, part)

    sum_start(2, lax.fori_loop(0, XS, residual_gram, jnp.zeros((K, K), F32)), snd.at[16])
    sum_spread(2, sum_middle(2), snd.at[17])
    gram1 = sum_end(2)
    mix = dot(gsrc[4], gram1)
    owned(1)
    gather_columns(1, cv)

    def image_of(wide, wider):
        return wide + dot(wide, mix) - dot(wider, step)

    b_own = rb[x, part_rows(z)]
    d_own = b_own - dot(own[0], step) + dot(b_own, mix)
    sum_start(3, dot_t(d_own, image_of(own[0], own[1])), snd.at[18])
    gz[z] = sum_middle(3)
    to_z(lambda t: (gz.at[z], gz.at[z]), snd.at[19], gz_sem)

    @pl.loop(1, ZS)
    def _(k):
        t = lax.rem(z + k, ZS)
        await_bytes(gz.at[t], gz_sem.at[t])

    total = gz[0]
    for j in range(1, ZS):
        total = total + gz[j]
    gx[x] = total
    to_x(lambda t: (gx.at[x], gx.at[x]), snd.at[20], gx_sem)

    @pl.loop(1, XS)
    def _(k):
        t = lax.rem(x + k, XS)
        await_bytes(gx.at[t], gx_sem.at[t])

    sum_spread(3, (gx[0] + gx[1]) + (gx[2] + gx[3]), snd.at[21])
    curvature2 = sum_end(3)
    step2 = dot(invert(curvature2), gfull[2])
    columns_here(1, cv)
    res = cb[...] - dot(cw[...], step)
    direction = res + dot(cb[...], mix)
    out_x[...] = dot(cb[...], step) + dot(direction, step2)
    out_r[...] = res - dot(image_of(cw[...], cv[...]), step2)

    small = 7 * GP
    for index, rows in (
        (0, 7 * PART), (1, 3 * SET), (2, 3 * SET), (3, 7 * PART), (4, 7 * PART),
        (5, 7 * PART), (6, 7 * PART), (7, 7 * PART), (8, 7 * PART), (9, 3 * SET),
        (10, small), (11, small), (12, 7 * PART), (13, 3 * SET), (14, small), (15, small),
        (16, small), (17, small), (18, small), (19, small), (20, 3 * GP), (21, small),
    ):
        await_sent(snd.at[index], rows)

    @pl.when(jnp.logical_not(diagonal))
    def _():
        for index in range(5):
            await_sent(snd0.at[index], PART)


def per_device(stored, rhs):
    vm = pltpu.VMEM
    dma = pltpu.SemaphoreType.DMA
    outs = pl.pallas_call(
        kernel,
        out_shape=(jax.ShapeDtypeStruct((SET, K), F32), jax.ShapeDtypeStruct((SET, K), F32)),
        in_specs=[pl.BlockSpec(memory_space=pl.ANY), pl.BlockSpec(memory_space=pl.ANY)],
        out_specs=(pl.BlockSpec(memory_space=pltpu.VMEM), pl.BlockSpec(memory_space=pltpu.VMEM)),
        scratch_shapes=[
            vm((NBC * XS * SET, BS), F32),
            vm((NBC, XS * BS, SET), BF16),
            vm((NBC, XS * BS, SET), BF16),
            vm((SET, K), F32),
            vm((SET, K), F32),
            vm((SET, K), F32),
            vm((SET, 2 * K), BF16),
            vm((XS, SET, K), F32),
            vm((XS, SET, K), F32),
            vm((NBC, 2 * K, XS * BS), BF16),
            vm((K, SET), F32),
            vm((2, XS, SET, K), F32),
            vm((2, XS, SET, K), F32),
            vm((2, SET, K), F32),
            vm((2, ZS, PART, K), F32),
            vm((2, SET, K), F32),
            vm((2, ROWS, PART, K), F32),
            vm((2, PART, K), F32),
            vm((5, K, K), F32),
            vm((4, ROWS, GP, K), F32),
            vm((4, K, K), F32),
            vm((ZS, GP, K), F32),
            vm((XS, GP, K), F32),
            vm((K, K), F32),
            dma((NBC + 1,)),
            dma((22,)),
            dma((5,)),
            dma((ROWS,)),
            dma((XS,)),
            dma((2, XS)),
            dma((2, ZS)),
            dma((2, ROWS)),
            dma((2, ZS)),
            dma((ZS,)),
            dma((XS,)),
            dma((4, ROWS)),
            dma((4, ROWS)),
            dma((ZS,)),
            dma((XS,)),
        ],
        compiler_params=pltpu.CompilerParams(
            collective_id=0, has_side_effects=True, vmem_limit_bytes=56 * 2**20
        ),
        name="block_cg",
    )(stored.reshape(-1, BS), rhs.reshape(-1, K))
    return tuple(o.reshape(rhs.shape) for o in outs)


def solution(mesh):
    return jax.shard_map(
        per_device,
        mesh=mesh,
        in_specs=(P(None, "row", None, None, "col", None), P(None, "col", None, None)),
        out_specs=(P(None, "col", None, None), P(None, "col", None, None)),
        check_vma=False,
    )
```

```python
import functools

import jax
import jax.numpy as jnp
from jax import lax
from jax.experimental import pallas as pl
from jax.experimental.pallas import tpu as pltpu
from jax.sharding import PartitionSpec as P

MESH = pl.DeviceIdType.MESH
HIGHEST = lax.Precision.HIGHEST
F32 = jnp.float32
BF16 = jnp.bfloat16

ROWS = 8
XS = 4
ZS = 8
NBC = 5
BS = 128
K = 128
SET = NBC * BS
PART = SET // ROWS
GP = K // ROWS
FOUR = 4
WIDE = 20


def dot(a, b):
    return jnp.dot(a, b, precision=HIGHEST, preferred_element_type=F32)


def dot_t(a, b):
    return lax.dot_general(
        a, b, (((0,), (0,)), ((), ())), precision=HIGHEST, preferred_element_type=F32
    )


def halves(value):
    high = value.astype(BF16)
    low = (value - high.astype(F32)).astype(BF16)
    return high, low


def kernel(
    stored, rhs, out_x, out_r,
    araw, ahi, alo, cb, cw, cv, chl, rb, rw, rt, yt,
    p, rx, q, rz, yv, ry, own, swapped,
    gsrc, grs, gfull, gz, gx, mat, cres, cdir, cimg,
    ld_sem, snd, snd0, rb_z, rb_x, x_sem, z_sem, y_sem, c_sem, w_sem, rw_z, rw_x,
    grs_sem, gag_sem, gz_sem, gx_sem,
):
    r = lax.axis_index("row")
    c = lax.axis_index("col")
    x = c // ZS
    z = lax.rem(c, ZS)
    diagonal = r == z

    def send(src, dst, ssem, rsem, row, xx, zz):
        pltpu.make_async_remote_copy(
            src_ref=src, dst_ref=dst, send_sem=ssem, recv_sem=rsem,
            device_id=(row, xx * ZS + zz), device_id_type=MESH,
        ).start()

    def await_bytes(ref, sem):
        pltpu.make_async_copy(ref, ref, sem).wait()

    def await_sent(sem, rows):
        part = araw.at[pl.ds(0, rows)]
        pltpu.make_async_copy(part, part, sem).wait()

    load_b = pltpu.make_async_copy(rhs, cb, ld_sem.at[NBC])
    load_b.start()
    span = XS * SET

    def load_a(b):
        rows = pl.ds(b * span, span)
        return pltpu.make_async_copy(stored.at[rows], araw.at[rows], ld_sem.at[b])

    for b in range(NBC):
        load_a(b).start()

    barrier = pltpu.get_barrier_semaphore()

    def greet(row, xx, zz):
        pl.semaphore_signal(barrier, inc=1, device_id=(row, xx * ZS + zz), device_id_type=MESH)

    @pl.loop(1, 8)
    def _(k):
        greet(r, x, lax.rem(z + k, ZS))
        greet(lax.rem(r + k, ROWS), x, z)
        greet(lax.rem(r + k, ROWS), x, r)

    @pl.loop(1, XS)
    def _(k):
        greet(r, lax.rem(x + k, XS), z)

    @pl.when(jnp.logical_not(diagonal))
    def _():
        greet(r, x, r)
        pl.semaphore_wait(barrier, 25)

    @pl.when(diagonal)
    def _():
        pl.semaphore_wait(barrier, 24)

    load_b.wait()

    def to_z(dst_of, sem, rsem):

        @pl.loop(1, ZS)
        def _(k):
            t = lax.rem(z + k, ZS)
            s_ref, d_ref = dst_of(t)
            send(s_ref, d_ref, sem, rsem.at[z], r, x, t)

    def to_x(dst_of, sem, rsem):
        @pl.loop(1, XS)
        def _(k):
            t = lax.rem(x + k, XS)
            s_ref, d_ref = dst_of(t)
            send(s_ref, d_ref, sem, rsem.at[x], r, t, z)

    def to_r(dst_of, sem, rsem):
        @pl.loop(1, ROWS)
        def _(k):
            t = lax.rem(r + k, ROWS)
            s_ref, d_ref = dst_of(t)
            send(s_ref, d_ref, sem, rsem.at[r], t, x, z)

    def with_own(first, rest, src, dst, ssem0, rsem):
        @pl.when(diagonal)
        def _():
            pltpu.make_async_copy(src, dst, rsem).start()

        @pl.when(jnp.logical_not(diagonal))
        def _():
            send(src, dst, ssem0, rsem, *first)

        rest()

    def to_cross(src_of, dst, ssem, ssem0, rsem):
        def rest():
            @pl.loop(1, ZS)
            def _(k):
                t = lax.rem(z + k, ZS)
                send(src_of(t), dst, ssem, rsem.at[r], z, x, t)

        with_own((z, x, z), rest, src_of(z), dst, ssem0, rsem.at[r])

    def part_rows(j):
        return pl.ds(pl.multiple_of(j * PART, 8), PART)

    def small_rows(j):
        return pl.ds(pl.multiple_of(j * GP, 8), GP)

    def split_columns(source):
        high, low = halves(source[...])
        chl[:, :K] = high
        chl[:, K:] = low

    def products_by_rows(m):
        for b in range(NBC):
            depth = (b + 1) * BS
            right = chl[:depth, :]
            both = jnp.dot(ahi[b, :, :depth], right, preferred_element_type=F32) + jnp.dot(
                alo[b, :, :depth], right, preferred_element_type=F32
            )
            total = both[:, :K] + both[:, K:]
            for xx in range(XS):
                p[m, xx, b * BS : (b + 1) * BS, :] = total[xx * BS : (xx + 1) * BS, :]

    def turn_rows(source):
        for b in range(NBC):

            @pl.loop(0, XS)
            def _(xx):
                high, low = halves(source[xx, b * BS : (b + 1) * BS, :].T)
                at = pl.ds(pl.multiple_of(xx * BS, BS), BS)
                rt[b, :K, at] = high
                rt[b, K:, at] = low

    def products_by_columns(m):
        for b in reversed(range(NBC)):
            depth = (b + 1) * BS
            left = rt[b]
            both = jnp.dot(left, ahi[b, :, :depth], preferred_element_type=F32) + jnp.dot(
                left, alo[b, :, :depth], preferred_element_type=F32
            )
            total = both[:K, :] + both[K:, :]
            if b == NBC - 1:
                yt[...] = total
            else:
                yt[:, :depth] += total
        for b in range(NBC):
            yv[m, b * BS : (b + 1) * BS, :] = yt[:, b * BS : (b + 1) * BS].T

    def gram_rows(left, right):
        def step(xx, total):
            return total + dot_t(left[xx], right[xx])

        return lax.fori_loop(0, XS, step, jnp.zeros((K, K), F32))

    lanes = lax.broadcasted_iota(jnp.int32, (K, K), 1)
    subs = lax.broadcasted_iota(jnp.int32, (K, K), 0)
    lane_row = lax.broadcasted_iota(jnp.int32, (1, K), 1)

    def eliminate(now, rows, first):
        hits = [lane_row == first + a for a in range(FOUR)]
        any_hit = hits[0] | hits[1] | hits[2] | hits[3]
        cols = [
            jnp.sum(jnp.where(lanes == first + a, now, 0.0), axis=1, keepdims=True)
            for a in range(FOUR)
        ]
        block = [
            [jnp.sum(jnp.where(h, row, 0.0), axis=1, keepdims=True) for h in hits] for row in rows
        ]
        rows = [
            jnp.where(any_hit, jnp.where(h, 1.0, 0.0), row) for h, row in zip(hits, rows)
        ]
        scale = []
        for a in range(FOUR):
            scale.append(1.0 / block[a][a])
            for b in range(a + 1, FOUR):
                factor = block[b][a] * scale[a]
                for c in range(a + 1, FOUR):
                    block[b][c] = block[b][c] - factor * block[a][c]
                rows[b] = rows[b] - factor * rows[a]
        for a in reversed(range(FOUR)):
            for b in range(a + 1, FOUR):
                rows[a] = rows[a] - block[a][b] * rows[b]
            rows[a] = rows[a] * scale[a]
        now = jnp.where((lanes >= first) & (lanes < first + FOUR), 0.0, now)
        for a in range(FOUR):
            now = now - cols[a] * rows[a]
        for a in range(FOUR):
            now = jnp.where(subs == first + a, rows[a], now)
        return now

    def pivots(slots, first, last):
        @pl.loop(first // FOUR, last // FOUR)
        def _(i):
            done = [
                eliminate(mat[s], [mat[s, pl.ds(FOUR * i + a, 1), :] for a in range(FOUR)], FOUR * i)
                for s in slots
            ]
            for s, value in zip(slots, done):
                mat[s] = value

    def sum_start(k, value, sem):
        gsrc[k] = value
        to_r(lambda t: (gsrc.at[k, small_rows(t)], grs.at[k, r]), sem, grs_sem.at[k])

    def sum_middle(k):
        grs[k, r] = gsrc[k, small_rows(r)]

        @pl.loop(1, ROWS)
        def _(j):
            t = lax.rem(r + j, ROWS)
            await_bytes(grs.at[k, t], grs_sem.at[k, t])

        total = grs[k, 0]
        for j in range(1, ROWS):
            total = total + grs[k, j]
        return total

    def sum_spread(k, total, sem):
        gfull[k, small_rows(r)] = total
        piece = gfull.at[k, small_rows(r)]
        to_r(lambda t: (piece, piece), sem, gag_sem.at[k])

    def sum_end(k):
        @pl.loop(1, ROWS)
        def _(j):
            t = lax.rem(r + j, ROWS)
            await_bytes(gfull.at[k, small_rows(t)], gag_sem.at[k, t])

        return gfull[k]

    def wide_z(k):
        gz[k, z] = sum_middle(k)
        to_z(lambda t: (gz.at[k, z], gz.at[k, z]), snd.at[WIDE + 2 * k], gz_sem.at[k])

    def wide_x(k):
        @pl.loop(1, ZS)
        def _(j):
            t = lax.rem(z + j, ZS)
            await_bytes(gz.at[k, t], gz_sem.at[k, t])

        total = gz[k, 0]
        for j in range(1, ZS):
            total = total + gz[k, j]
        gx[k, x] = total
        to_x(lambda t: (gx.at[k, x], gx.at[k, x]), snd.at[WIDE + 1 + 2 * k], gx_sem.at[k])

    def wide_r(k, sem):
        @pl.loop(1, XS)
        def _(j):
            t = lax.rem(x + j, XS)
            await_bytes(gx.at[k, t], gx_sem.at[k, t])

        sum_spread(k, (gx[k, 0] + gx[k, 1]) + (gx[k, 2] + gx[k, 3]), sem)

    to_cross(
        lambda t: cb.at[part_rows(r)], rb.at[x, part_rows(r)], snd.at[0], snd0.at[0], rb_z
    )
    split_columns(cb)

    mine = x * ZS + z
    for b in range(NBC):
        load_a(b).wait()

        @pl.loop(0, XS)
        def _(xx):
            there = xx * ZS + r
            weight = jnp.where(there > mine, 1.0, jnp.where(there == mine, 0.5, 0.0)).astype(F32)
            at = pl.ds(pl.multiple_of(xx * BS, BS), BS)
            for bb in range(b + 1):
                block = araw[pl.ds((b * XS + xx) * SET + bb, BS, NBC), :]
                if bb == b:
                    block = block * weight
                high, low = halves(block)
                ahi[b, at, bb * BS : (bb + 1) * BS] = high
                alo[b, at, bb * BS : (bb + 1) * BS] = low

    def scatter_rows(m):
        @pl.loop(1, ZS + 1)
        def _(k):
            at = part_rows(lax.rem(z + k, ZS))
            sem = x_sem.at[m, x, lax.rem(z + k, ZS)]
            for far in (1, 3, 2):
                t = lax.rem(x + far, XS)
                send(p.at[m, t, at], rx.at[m, x, at], snd.at[1 + m], sem, r, t, z)

    def sum_x(m, slot):
        at = part_rows(slot)
        total = p[m, x, at]
        for far in (1, 3, 2):
            t = lax.rem(x + far, XS)
            await_bytes(rx.at[m, t, at], x_sem.at[m, t, slot])
            total = total + rx[m, t, at]
        return total

    def scatter_rows_next(m, first, last):
        @pl.loop(first, last)
        def _(k):
            slot = lax.rem(z + k, ZS)
            q[m, part_rows(slot)] = sum_x(m, slot)
            send(
                q.at[m, part_rows(slot)], rz.at[m, z], snd.at[3 + m], z_sem.at[m, z], r, x, slot
            )

    def scatter_columns(m):
        to_cross(
            lambda t: yv.at[m, part_rows(t)], ry.at[m, r], snd.at[5 + m], snd0.at[1 + m], y_sem.at[m]
        )

    def owned(m):
        rz[m, z] = sum_x(m, z)

        @pl.loop(1, ZS)
        def _(k):
            t = lax.rem(z + k, ZS)
            await_bytes(rz.at[m, t], z_sem.at[m, t])

        @pl.loop(0, ROWS)
        def _(k):
            await_bytes(ry.at[m, k], y_sem.at[m, k])

        total = rz[m, 0] + ry[m, 0]
        for j in range(1, 8):
            total = total + (rz[m, j] + ry[m, j])
        own[m] = total

    def swap_start(m):
        @pl.when(diagonal)
        def _():
            swapped[m] = own[m]

        @pl.when(jnp.logical_not(diagonal))
        def _():
            send(own.at[m], swapped.at[m], snd0.at[3 + m], w_sem.at[m], z, x, r)

    def swap_spread(m, dst):
        @pl.when(jnp.logical_not(diagonal))
        def _():
            await_bytes(swapped.at[m], w_sem.at[m])

        dst[part_rows(r)] = swapped[m]
        piece = dst.at[part_rows(r)]
        to_r(lambda t: (piece, piece), snd.at[7 + m], c_sem.at[m])

    def columns_here(m, dst):
        @pl.loop(1, ROWS)
        def _(k):
            t = lax.rem(r + k, ROWS)
            await_bytes(dst.at[part_rows(t)], c_sem.at[m, t])

    def forward(rows, slot, ssem, rsem):
        piece = rows.at[x, part_rows(slot)]
        for far in (1, 3, 2):
            send(piece, piece, ssem, rsem.at[x], r, lax.rem(x + far, XS), z)

    def rows_here(rows, rsem):
        @pl.loop(1, XS)
        def _(k):
            t = lax.rem(x + k, XS)
            await_bytes(rows.at[t], rsem.at[t])

    products_by_rows(0)

    @pl.loop(0, ROWS)
    def _(k):
        slot = lax.rem(r + k, ROWS)
        await_bytes(rb.at[x, part_rows(slot)], rb_z.at[slot])
        forward(rb, slot, snd.at[9], rb_x)

    scatter_rows(0)
    rows_here(rb, rb_x)
    turn_rows(rb)
    products_by_columns(0)
    scatter_columns(0)
    sum_start(1, gram_rows(rb, p.at[0]), snd.at[14])
    sum_start(0, gram_rows(rb, rb), snd.at[10])
    scatter_rows_next(0, 1, 3)
    wide_z(1)
    sum_spread(0, sum_middle(0), snd.at[11])
    scatter_rows_next(0, 3, 5)
    wide_x(1)
    scatter_rows_next(0, 5, 7)
    wide_r(1, snd.at[15])
    scatter_rows_next(0, 7, 8)
    owned(0)

    swap_start(0)
    rw[x, part_rows(z)] = own[0]
    to_z(lambda t: (own.at[0], rw.at[x, part_rows(z)]), snd.at[12], rw_z)
    forward(rw, z, snd.at[13], rw_x)
    mat[0] = sum_end(0)
    half = sum_end(1)
    mat[1] = half + half.T

    def onward(k):
        slot = lax.rem(z + k, ZS)
        await_bytes(rw.at[x, part_rows(slot)], rw_z.at[slot])
        forward(rw, slot, snd.at[13], rw_x)

    chunk = K // 8
    for k, far in enumerate((1, 7, 2, 6, 3, 5, 4)):
        onward(far)
        if k == 3:
            swap_spread(0, cw)
        pivots((0, 1), k * chunk, (k + 1) * chunk)
    columns_here(0, cw)
    split_columns(cw)
    products_by_rows(1)
    scatter_rows(1)
    pivots((0, 1), K - chunk, K)
    step = dot(mat[1], gfull[0])
    b_own = rb[x, part_rows(z)]
    r_own = b_own - dot(own[0], step)
    sum_start(2, dot_t(r_own, r_own), snd.at[16])
    rows_here(rw, rw_x)
    turn_rows(rw)
    wide_z(2)
    products_by_columns(1)
    scatter_columns(1)
    scatter_rows_next(1, 1, 2)
    wide_x(2)
    scatter_rows_next(1, 2, 4)
    wide_r(2, snd.at[17])
    scatter_rows_next(1, 4, 8)
    mix = dot(mat[0], sum_end(2))
    owned(1)
    swap_start(1)

    def image_of(wide, wider):
        return wide + dot(wide, mix) - dot(wider, step)

    d_own = r_own + dot(b_own, mix)
    sum_start(3, dot_t(d_own, image_of(own[0], own[1])), snd.at[18])
    res = cb[...] - dot(cw[...], step)
    cres[...] = res
    cdir[...] = res + dot(cb[...], mix)
    wide_z(3)
    swap_spread(1, cv)
    wide_x(3)
    out_x[...] = dot(cb[...], step)
    wide_r(3, snd.at[19])
    columns_here(1, cv)
    cimg[...] = image_of(cw[...], cv[...])
    mat[0] = sum_end(3)
    pivots((0,), 0, K)
    step2 = dot(mat[0], gfull[2])
    out_x[...] += dot(cdir[...], step2)
    out_r[...] = cres[...] - dot(cimg[...], step2)

    small = 7 * GP
    wide = tuple((WIDE + 2 * k + j, rows) for k in (1, 2, 3) for j, rows in ((0, small), (1, 3 * GP)))
    for index, rows in wide + (
        (0, 7 * PART), (1, 3 * SET), (2, 3 * SET), (3, 7 * PART), (4, 7 * PART),
        (5, 7 * PART), (6, 7 * PART), (7, 7 * PART), (8, 7 * PART), (9, 3 * SET),
        (10, small), (11, small), (12, 7 * PART), (13, 3 * SET), (14, small), (15, small),
        (16, small), (17, small), (18, small), (19, small),
    ):
        await_sent(snd.at[index], rows)

    @pl.when(jnp.logical_not(diagonal))
    def _():
        for index in range(5):
            await_sent(snd0.at[index], PART)


def per_device(stored, rhs):
    vm = pltpu.VMEM
    dma = pltpu.SemaphoreType.DMA
    outs = pl.pallas_call(
        kernel,
        out_shape=(jax.ShapeDtypeStruct((SET, K), F32), jax.ShapeDtypeStruct((SET, K), F32)),
        in_specs=[pl.BlockSpec(memory_space=pl.ANY), pl.BlockSpec(memory_space=pl.ANY)],
        out_specs=(pl.BlockSpec(memory_space=pltpu.VMEM), pl.BlockSpec(memory_space=pltpu.VMEM)),
        scratch_shapes=[
            vm((NBC * XS * SET, BS), F32),
            vm((NBC, XS * BS, SET), BF16),
            vm((NBC, XS * BS, SET), BF16),
            vm((SET, K), F32),
            vm((SET, K), F32),
            vm((SET, K), F32),
            vm((SET, 2 * K), BF16),
            vm((XS, SET, K), F32),
            vm((XS, SET, K), F32),
            vm((NBC, 2 * K, XS * BS), BF16),
            vm((K, SET), F32),
            vm((2, XS, SET, K), F32),
            vm((2, XS, SET, K), F32),
            vm((2, SET, K), F32),
            vm((2, ZS, PART, K), F32),
            vm((2, SET, K), F32),
            vm((2, ROWS, PART, K), F32),
            vm((2, PART, K), F32),
            vm((2, PART, K), F32),
            vm((4, K, K), F32),
            vm((4, ROWS, GP, K), F32),
            vm((4, K, K), F32),
            vm((4, ZS, GP, K), F32),
            vm((4, XS, GP, K), F32),
            vm((2, K, K), F32),
            vm((SET, K), F32),
            vm((SET, K), F32),
            vm((SET, K), F32),
            dma((NBC + 1,)),
            dma((28,)),
            dma((5,)),
            dma((ROWS,)),
            dma((XS,)),
            dma((2, XS, ZS)),
            dma((2, ZS)),
            dma((2, ROWS)),
            dma((2, ROWS)),
            dma((2,)),
            dma((ZS,)),
            dma((XS,)),
            dma((4, ROWS)),
            dma((4, ROWS)),
            dma((4, ZS)),
            dma((4, XS)),
        ],
        compiler_params=pltpu.CompilerParams(
            collective_id=0, has_side_effects=True, vmem_limit_bytes=56 * 2**20
        ),
        name="block_cg",
    )(stored.reshape(-1, BS), rhs.reshape(-1, K))
    return tuple(o.reshape(rhs.shape) for o in outs)


def solution(mesh):
    return jax.shard_map(
        per_device,
        mesh=mesh,
        in_specs=(P(None, "row", None, None, "col", None), P(None, "col", None, None)),
        out_specs=(P(None, "col", None, None), P(None, "col", None, None)),
        check_vma=False,
    )
```

```python
import functools

import jax
import jax.numpy as jnp
from jax import lax
from jax.experimental import pallas as pl
from jax.experimental.pallas import tpu as pltpu
from jax.sharding import PartitionSpec as P

MESH = pl.DeviceIdType.MESH
HIGHEST = lax.Precision.HIGHEST
F32 = jnp.float32
BF16 = jnp.bfloat16

ROWS = 8
XS = 4
ZS = 8
NBC = 5
BS = 128
K = 128
SET = NBC * BS
PART = SET // ROWS
GP = K // ROWS
FOUR = 4
WIDE = 20


def dot(a, b):
    return jnp.dot(a, b, precision=HIGHEST, preferred_element_type=F32)


def dot_t(a, b):
    return lax.dot_general(
        a, b, (((0,), (0,)), ((), ())), precision=HIGHEST, preferred_element_type=F32
    )


def halves(value):
    high = value.astype(BF16)
    low = (value - high.astype(F32)).astype(BF16)
    return high, low


def kernel(
    stored, rhs, out_x, out_r,
    araw, ahi, alo, cb, cw, cv, chl, rb, rw, rt, yt,
    p, rx, q, rz, yv, ry, own, swapped,
    gsrc, grs, gfull, gz, gx, mat, cres, cdir, cimg,
    ld_sem, snd, snd0, rb_z, rb_x, x_sem, z_sem, y_sem, c_sem, w_sem, rw_z, rw_x,
    grs_sem, gag_sem, gz_sem, gx_sem,
):
    r = lax.axis_index("row")
    c = lax.axis_index("col")
    x = c // ZS
    z = lax.rem(c, ZS)
    diagonal = r == z

    def send(src, dst, ssem, rsem, row, xx, zz):
        pltpu.make_async_remote_copy(
            src_ref=src, dst_ref=dst, send_sem=ssem, recv_sem=rsem,
            device_id=(row, xx * ZS + zz), device_id_type=MESH,
        ).start()

    def await_bytes(ref, sem):
        pltpu.make_async_copy(ref, ref, sem).wait()

    def await_sent(sem, rows):
        part = araw.at[pl.ds(0, rows)]
        pltpu.make_async_copy(part, part, sem).wait()

    load_b = pltpu.make_async_copy(rhs, cb, ld_sem.at[NBC])
    load_b.start()
    span = XS * SET

    def load_a(b):
        rows = pl.ds(b * span, span)
        return pltpu.make_async_copy(stored.at[rows], araw.at[rows], ld_sem.at[b])

    for b in range(NBC):
        load_a(b).start()

    barrier = pltpu.get_barrier_semaphore()

    def greet(row, xx, zz):
        pl.semaphore_signal(barrier, inc=1, device_id=(row, xx * ZS + zz), device_id_type=MESH)

    @pl.loop(1, 8)
    def _(k):
        greet(r, x, lax.rem(z + k, ZS))
        greet(lax.rem(r + k, ROWS), x, z)
        greet(lax.rem(r + k, ROWS), x, r)

    @pl.loop(1, XS)
    def _(k):
        greet(r, lax.rem(x + k, XS), z)

    @pl.when(jnp.logical_not(diagonal))
    def _():
        greet(r, x, r)
        pl.semaphore_wait(barrier, 25)

    @pl.when(diagonal)
    def _():
        pl.semaphore_wait(barrier, 24)

    load_b.wait()

    def to_z(dst_of, sem, rsem):

        @pl.loop(1, ZS)
        def _(k):
            t = lax.rem(z + k, ZS)
            s_ref, d_ref = dst_of(t)
            send(s_ref, d_ref, sem, rsem.at[z], r, x, t)

    def to_x(dst_of, sem, rsem):
        @pl.loop(1, XS)
        def _(k):
            t = lax.rem(x + k, XS)
            s_ref, d_ref = dst_of(t)
            send(s_ref, d_ref, sem, rsem.at[x], r, t, z)

    def to_r(dst_of, sem, rsem):
        @pl.loop(1, ROWS)
        def _(k):
            t = lax.rem(r + k, ROWS)
            s_ref, d_ref = dst_of(t)
            send(s_ref, d_ref, sem, rsem.at[r], t, x, z)

    def with_own(first, rest, src, dst, ssem0, rsem):
        @pl.when(diagonal)
        def _():
            pltpu.make_async_copy(src, dst, rsem).start()

        @pl.when(jnp.logical_not(diagonal))
        def _():
            send(src, dst, ssem0, rsem, *first)

        rest()

    def to_cross(src_of, dst, ssem, ssem0, rsem):
        def rest():
            @pl.loop(1, ZS)
            def _(k):
                t = lax.rem(z + k, ZS)
                send(src_of(t), dst, ssem, rsem.at[r], z, x, t)

        with_own((z, x, z), rest, src_of(z), dst, ssem0, rsem.at[r])

    def part_rows(j):
        return pl.ds(pl.multiple_of(j * PART, 8), PART)

    def small_rows(j):
        return pl.ds(pl.multiple_of(j * GP, 8), GP)

    def split_columns(source):
        high, low = halves(source[...])
        chl[:, :K] = high
        chl[:, K:] = low

    def products_by_rows(m):
        for b in range(NBC):
            depth = (b + 1) * BS
            right = chl[:depth, :]
            both = jnp.dot(ahi[b, :, :depth], right, preferred_element_type=F32) + jnp.dot(
                alo[b, :, :depth], right, preferred_element_type=F32
            )
            total = both[:, :K] + both[:, K:]
            for xx in range(XS):
                p[m, xx, b * BS : (b + 1) * BS, :] = total[xx * BS : (xx + 1) * BS, :]

    def turn_rows(source):
        for b in range(NBC):

            @pl.loop(0, XS)
            def _(xx):
                high, low = halves(source[xx, b * BS : (b + 1) * BS, :].T)
                at = pl.ds(pl.multiple_of(xx * BS, BS), BS)
                rt[b, :K, at] = high
                rt[b, K:, at] = low

    def products_by_columns(m):
        for b in reversed(range(NBC)):
            depth = (b + 1) * BS
            left = rt[b]
            both = jnp.dot(left, ahi[b, :, :depth], preferred_element_type=F32) + jnp.dot(
                left, alo[b, :, :depth], preferred_element_type=F32
            )
            total = both[:K, :] + both[K:, :]
            if b == NBC - 1:
                yt[...] = total
            else:
                yt[:, :depth] += total
        for b in range(NBC):
            yv[m, b * BS : (b + 1) * BS, :] = yt[:, b * BS : (b + 1) * BS].T

    def gram_rows(left, right):
        def step(xx, total):
            return total + dot_t(left[xx], right[xx])

        return lax.fori_loop(0, XS, step, jnp.zeros((K, K), F32))

    lanes = lax.broadcasted_iota(jnp.int32, (K, K), 1)
    subs = lax.broadcasted_iota(jnp.int32, (K, K), 0)
    lane_row = lax.broadcasted_iota(jnp.int32, (1, K), 1)

    def eliminate(now, rows, first):
        hits = [lane_row == first + a for a in range(FOUR)]
        any_hit = hits[0] | hits[1] | hits[2] | hits[3]
        cols = [
            jnp.sum(jnp.where(lanes == first + a, now, 0.0), axis=1, keepdims=True)
            for a in range(FOUR)
        ]
        block = [
            [jnp.sum(jnp.where(h, row, 0.0), axis=1, keepdims=True) for h in hits] for row in rows
        ]
        rows = [
            jnp.where(any_hit, jnp.where(h, 1.0, 0.0), row) for h, row in zip(hits, rows)
        ]
        scale = []
        for a in range(FOUR):
            scale.append(1.0 / block[a][a])
            for b in range(a + 1, FOUR):
                factor = block[b][a] * scale[a]
                for c in range(a + 1, FOUR):
                    block[b][c] = block[b][c] - factor * block[a][c]
                rows[b] = rows[b] - factor * rows[a]
        for a in reversed(range(FOUR)):
            for b in range(a + 1, FOUR):
                rows[a] = rows[a] - block[a][b] * rows[b]
            rows[a] = rows[a] * scale[a]
        now = jnp.where((lanes >= first) & (lanes < first + FOUR), 0.0, now)
        for a in range(FOUR):
            now = now - cols[a] * rows[a]
        for a in range(FOUR):
            now = jnp.where(subs == first + a, rows[a], now)
        return now

    def pivots(slots, first, last):
        @pl.loop(first // FOUR, last // FOUR)
        def _(i):
            done = [
                eliminate(mat[s], [mat[s, pl.ds(FOUR * i + a, 1), :] for a in range(FOUR)], FOUR * i)
                for s in slots
            ]
            for s, value in zip(slots, done):
                mat[s] = value

    def sum_start(k, value, sem):
        gsrc[k] = value
        to_r(lambda t: (gsrc.at[k, small_rows(t)], grs.at[k, r]), sem, grs_sem.at[k])

    def sum_middle(k):
        grs[k, r] = gsrc[k, small_rows(r)]

        @pl.loop(1, ROWS)
        def _(j):
            t = lax.rem(r + j, ROWS)
            await_bytes(grs.at[k, t], grs_sem.at[k, t])

        total = grs[k, 0]
        for j in range(1, ROWS):
            total = total + grs[k, j]
        return total

    def sum_spread(k, total, sem):
        gfull[k, small_rows(r)] = total
        piece = gfull.at[k, small_rows(r)]
        to_r(lambda t: (piece, piece), sem, gag_sem.at[k])

    def sum_end(k):
        @pl.loop(1, ROWS)
        def _(j):
            t = lax.rem(r + j, ROWS)
            await_bytes(gfull.at[k, small_rows(t)], gag_sem.at[k, t])

        return gfull[k]

    def wide_z(k):
        gz[k, z] = sum_middle(k)
        to_z(lambda t: (gz.at[k, z], gz.at[k, z]), snd.at[WIDE + 2 * k], gz_sem.at[k])

    def wide_x(k):
        @pl.loop(1, ZS)
        def _(j):
            t = lax.rem(z + j, ZS)
            await_bytes(gz.at[k, t], gz_sem.at[k, t])

        total = gz[k, 0]
        for j in range(1, ZS):
            total = total + gz[k, j]
        gx[k, x] = total
        to_x(lambda t: (gx.at[k, x], gx.at[k, x]), snd.at[WIDE + 1 + 2 * k], gx_sem.at[k])

    def wide_r(k, sem):
        @pl.loop(1, XS)
        def _(j):
            t = lax.rem(x + j, XS)
            await_bytes(gx.at[k, t], gx_sem.at[k, t])

        sum_spread(k, (gx[k, 0] + gx[k, 1]) + (gx[k, 2] + gx[k, 3]), sem)

    to_cross(
        lambda t: cb.at[part_rows(r)], rb.at[x, part_rows(r)], snd.at[0], snd0.at[0], rb_z
    )
    split_columns(cb)

    mine = x * ZS + z
    for b in range(NBC):
        load_a(b).wait()

        @pl.loop(0, XS)
        def _(xx):
            there = xx * ZS + r
            weight = jnp.where(there > mine, 1.0, jnp.where(there == mine, 0.5, 0.0)).astype(F32)
            at = pl.ds(pl.multiple_of(xx * BS, BS), BS)
            for bb in range(b + 1):
                block = araw[pl.ds((b * XS + xx) * SET + bb, BS, NBC), :]
                if bb == b:
                    block = block * weight
                high, low = halves(block)
                ahi[b, at, bb * BS : (bb + 1) * BS] = high
                alo[b, at, bb * BS : (bb + 1) * BS] = low

    def scatter_rows(m, first, last):
        @pl.loop(first, last)
        def _(k):
            at = part_rows(lax.rem(z + k, ZS))
            sem = x_sem.at[m, x, lax.rem(z + k, ZS)]
            for far in (1, 3, 2):
                t = lax.rem(x + far, XS)
                send(p.at[m, t, at], rx.at[m, x, at], snd.at[1 + m], sem, r, t, z)

    def sum_x(m, slot):
        at = part_rows(slot)
        total = p[m, x, at]
        for far in (1, 3, 2):
            t = lax.rem(x + far, XS)
            await_bytes(rx.at[m, t, at], x_sem.at[m, t, slot])
            total = total + rx[m, t, at]
        return total

    def scatter_rows_next(m, first, last):
        @pl.loop(first, last)
        def _(k):
            slot = lax.rem(z + k, ZS)
            q[m, part_rows(slot)] = sum_x(m, slot)
            send(
                q.at[m, part_rows(slot)], rz.at[m, z], snd.at[3 + m], z_sem.at[m, z], r, x, slot
            )

    def scatter_columns(m):
        to_cross(
            lambda t: yv.at[m, part_rows(t)], ry.at[m, r], snd.at[5 + m], snd0.at[1 + m], y_sem.at[m]
        )

    def owned(m):
        rz[m, z] = sum_x(m, z)

        @pl.loop(1, ZS)
        def _(k):
            t = lax.rem(z + k, ZS)
            await_bytes(rz.at[m, t], z_sem.at[m, t])

        @pl.loop(0, ROWS)
        def _(k):
            await_bytes(ry.at[m, k], y_sem.at[m, k])

        total = rz[m, 0] + ry[m, 0]
        for j in range(1, 8):
            total = total + (rz[m, j] + ry[m, j])
        own[m] = total

    def swap_start(m):
        @pl.when(diagonal)
        def _():
            swapped[m] = own[m]

        @pl.when(jnp.logical_not(diagonal))
        def _():
            send(own.at[m], swapped.at[m], snd0.at[3 + m], w_sem.at[m], z, x, r)

    def swap_spread(m, dst):
        @pl.when(jnp.logical_not(diagonal))
        def _():
            await_bytes(swapped.at[m], w_sem.at[m])

        dst[part_rows(r)] = swapped[m]
        piece = dst.at[part_rows(r)]
        to_r(lambda t: (piece, piece), snd.at[7 + m], c_sem.at[m])

    def columns_here(m, dst):
        @pl.loop(1, ROWS)
        def _(k):
            t = lax.rem(r + k, ROWS)
            await_bytes(dst.at[part_rows(t)], c_sem.at[m, t])

    def forward(rows, slot, ssem, rsem):
        piece = rows.at[x, part_rows(slot)]
        for far in (1, 3, 2):
            send(piece, piece, ssem, rsem.at[x], r, lax.rem(x + far, XS), z)

    def rows_here(rows, rsem):
        @pl.loop(1, XS)
        def _(k):
            t = lax.rem(x + k, XS)
            await_bytes(rows.at[t], rsem.at[t])

    products_by_rows(0)
    scatter_rows(0, 1, 3)

    @pl.loop(0, ROWS)
    def _(k):
        slot = lax.rem(r + k, ROWS)
        await_bytes(rb.at[x, part_rows(slot)], rb_z.at[slot])
        forward(rb, slot, snd.at[9], rb_x)

    rows_here(rb, rb_x)
    scatter_rows(0, 3, ZS + 1)
    turn_rows(rb)
    products_by_columns(0)
    scatter_columns(0)
    sum_start(1, gram_rows(rb, p.at[0]), snd.at[14])
    sum_start(0, gram_rows(rb, rb), snd.at[10])
    scatter_rows_next(0, 1, 4)
    wide_z(1)
    sum_spread(0, sum_middle(0), snd.at[11])
    scatter_rows_next(0, 4, 8)
    mat[0] = sum_end(0)
    wide_x(1)
    owned(0)

    swap_start(0)
    rw[x, part_rows(z)] = own[0]
    to_z(lambda t: (own.at[0], rw.at[x, part_rows(z)]), snd.at[12], rw_z)
    forward(rw, z, snd.at[13], rw_x)
    wide_r(1, snd.at[15])

    def onward(k):
        slot = lax.rem(z + k, ZS)
        await_bytes(rw.at[x, part_rows(slot)], rw_z.at[slot])
        forward(rw, slot, snd.at[13], rw_x)

    chunk = K // 4
    for k, far in enumerate((1, 7, 2, 6, 3, 5, 4)):
        onward(far)
        if k == 3:
            swap_spread(0, cw)
            half = sum_end(1)
            mat[1] = half + half.T
        part = k % 4 * chunk
        pivots((k // 4,), part, part + chunk)
    columns_here(0, cw)
    split_columns(cw)
    products_by_rows(1)
    scatter_rows(1, 1, ZS + 1)
    pivots((1,), K - chunk, K)
    step = dot(mat[1], gfull[0])
    rows_here(rw, rw_x)
    turn_rows(rw)
    products_by_columns(1)
    scatter_columns(1)
    scatter_rows_next(1, 1, 3)

    def residual_gram(xx, total):
        part = rb[xx] - dot(rw[xx], step)
        return total + dot_t(part, part)

    sum_start(2, lax.fori_loop(0, XS, residual_gram, jnp.zeros((K, K), F32)), snd.at[16])
    scatter_rows_next(1, 3, 6)
    sum_spread(2, sum_middle(2), snd.at[17])
    scatter_rows_next(1, 6, 8)
    owned(1)
    swap_start(1)
    mix = dot(mat[0], sum_end(2))
    b_own = rb[x, part_rows(z)]
    r_own = b_own - dot(own[0], step)

    def image_of(wide, wider):
        return wide + dot(wide, mix) - dot(wider, step)

    d_own = r_own + dot(b_own, mix)
    sum_start(3, dot_t(d_own, image_of(own[0], own[1])), snd.at[18])
    res = cb[...] - dot(cw[...], step)
    cres[...] = res
    cdir[...] = res + dot(cb[...], mix)
    wide_z(3)
    swap_spread(1, cv)
    wide_x(3)
    out_x[...] = dot(cb[...], step)
    wide_r(3, snd.at[19])
    columns_here(1, cv)
    cimg[...] = image_of(cw[...], cv[...])
    mat[0] = sum_end(3)
    pivots((0,), 0, K)
    step2 = dot(mat[0], gfull[2])
    out_x[...] += dot(cdir[...], step2)
    out_r[...] = cres[...] - dot(cimg[...], step2)

    small = 7 * GP
    wide = tuple((WIDE + 2 * k + j, rows) for k in (1, 3) for j, rows in ((0, small), (1, 3 * GP)))
    for index, rows in wide + (
        (0, 7 * PART), (1, 3 * SET), (2, 3 * SET), (3, 7 * PART), (4, 7 * PART),
        (5, 7 * PART), (6, 7 * PART), (7, 7 * PART), (8, 7 * PART), (9, 3 * SET),
        (10, small), (11, small), (12, 7 * PART), (13, 3 * SET), (14, small), (15, small),
        (16, small), (17, small), (18, small), (19, small),
    ):
        await_sent(snd.at[index], rows)

    @pl.when(jnp.logical_not(diagonal))
    def _():
        for index in range(5):
            await_sent(snd0.at[index], PART)


def per_device(stored, rhs):
    vm = pltpu.VMEM
    dma = pltpu.SemaphoreType.DMA
    outs = pl.pallas_call(
        kernel,
        out_shape=(jax.ShapeDtypeStruct((SET, K), F32), jax.ShapeDtypeStruct((SET, K), F32)),
        in_specs=[pl.BlockSpec(memory_space=pl.ANY), pl.BlockSpec(memory_space=pl.ANY)],
        out_specs=(pl.BlockSpec(memory_space=pltpu.VMEM), pl.BlockSpec(memory_space=pltpu.VMEM)),
        scratch_shapes=[
            vm((NBC * XS * SET, BS), F32),
            vm((NBC, XS * BS, SET), BF16),
            vm((NBC, XS * BS, SET), BF16),
            vm((SET, K), F32),
            vm((SET, K), F32),
            vm((SET, K), F32),
            vm((SET, 2 * K), BF16),
            vm((XS, SET, K), F32),
            vm((XS, SET, K), F32),
            vm((NBC, 2 * K, XS * BS), BF16),
            vm((K, SET), F32),
            vm((2, XS, SET, K), F32),
            vm((2, XS, SET, K), F32),
            vm((2, SET, K), F32),
            vm((2, ZS, PART, K), F32),
            vm((2, SET, K), F32),
            vm((2, ROWS, PART, K), F32),
            vm((2, PART, K), F32),
            vm((2, PART, K), F32),
            vm((4, K, K), F32),
            vm((4, ROWS, GP, K), F32),
            vm((4, K, K), F32),
            vm((4, ZS, GP, K), F32),
            vm((4, XS, GP, K), F32),
            vm((2, K, K), F32),
            vm((SET, K), F32),
            vm((SET, K), F32),
            vm((SET, K), F32),
            dma((NBC + 1,)),
            dma((28,)),
            dma((5,)),
            dma((ROWS,)),
            dma((XS,)),
            dma((2, XS, ZS)),
            dma((2, ZS)),
            dma((2, ROWS)),
            dma((2, ROWS)),
            dma((2,)),
            dma((ZS,)),
            dma((XS,)),
            dma((4, ROWS)),
            dma((4, ROWS)),
            dma((4, ZS)),
            dma((4, XS)),
        ],
        compiler_params=pltpu.CompilerParams(
            collective_id=0, has_side_effects=True, vmem_limit_bytes=56 * 2**20
        ),
        name="block_cg",
    )(stored.reshape(-1, BS), rhs.reshape(-1, K))
    return tuple(o.reshape(rhs.shape) for o in outs)


def solution(mesh):
    return jax.shard_map(
        per_device,
        mesh=mesh,
        in_specs=(P(None, "row", None, None, "col", None), P(None, "col", None, None)),
        out_specs=(P(None, "col", None, None), P(None, "col", None, None)),
        check_vma=False,
    )
```

```python
import functools

import jax
import jax.numpy as jnp
from jax import lax
from jax.experimental import pallas as pl
from jax.experimental.pallas import tpu as pltpu
from jax.sharding import PartitionSpec as P

MESH = pl.DeviceIdType.MESH
HIGHEST = lax.Precision.HIGHEST
F32 = jnp.float32
BF16 = jnp.bfloat16

ROWS = 8
XS = 4
ZS = 8
NBC = 5
BS = 128
K = 128
SET = NBC * BS
PART = SET // ROWS
GP = K // ROWS
FOUR = 4
WIDE = 20


def dot(a, b):
    return jnp.dot(a, b, precision=HIGHEST, preferred_element_type=F32)


def dot_t(a, b):
    return lax.dot_general(
        a, b, (((0,), (0,)), ((), ())), precision=HIGHEST, preferred_element_type=F32
    )


def halves(value):
    high = value.astype(BF16)
    low = (value - high.astype(F32)).astype(BF16)
    return high, low


def kernel(
    stored, rhs, out_x, out_r,
    araw, ahi, alo, cb, cw, cv, chl, rb, rw, rt, yt,
    p, rx, q, rz, yv, ry, ysum, ycross, own, swapped,
    gsrc, grs, gfull, gz, gx, mat, cres, cdir, cimg,
    ld_sem, snd, snd0, rb_z, rb_x, x_sem, z_sem, y_sem, c_sem, w_sem, yx_sem, rw_z, rw_x,
    grs_sem, gag_sem, gz_sem, gx_sem,
):
    r = lax.axis_index("row")
    c = lax.axis_index("col")
    x = c // ZS
    z = lax.rem(c, ZS)
    diagonal = r == z

    def send(src, dst, ssem, rsem, row, xx, zz):
        pltpu.make_async_remote_copy(
            src_ref=src, dst_ref=dst, send_sem=ssem, recv_sem=rsem,
            device_id=(row, xx * ZS + zz), device_id_type=MESH,
        ).start()

    def await_bytes(ref, sem):
        pltpu.make_async_copy(ref, ref, sem).wait()

    def await_sent(sem, rows):
        part = araw.at[pl.ds(0, rows)]
        pltpu.make_async_copy(part, part, sem).wait()

    load_b = pltpu.make_async_copy(rhs, cb, ld_sem.at[NBC])
    load_b.start()
    span = XS * SET

    def load_a(b):
        rows = pl.ds(b * span, span)
        return pltpu.make_async_copy(stored.at[rows], araw.at[rows], ld_sem.at[b])

    for b in range(NBC):
        load_a(b).start()

    barrier = pltpu.get_barrier_semaphore()

    def greet(row, xx, zz):
        pl.semaphore_signal(barrier, inc=1, device_id=(row, xx * ZS + zz), device_id_type=MESH)

    @pl.loop(1, 8)
    def _(k):
        greet(r, x, lax.rem(z + k, ZS))
        greet(lax.rem(r + k, ROWS), x, z)
        greet(lax.rem(r + k, ROWS), x, r)

    @pl.loop(1, XS)
    def _(k):
        greet(r, lax.rem(x + k, XS), z)

    @pl.when(jnp.logical_not(diagonal))
    def _():
        greet(r, x, r)

    load_b.wait()

    def to_z(dst_of, sem, rsem):

        @pl.loop(1, ZS)
        def _(k):
            t = lax.rem(z + k, ZS)
            s_ref, d_ref = dst_of(t)
            send(s_ref, d_ref, sem, rsem.at[z], r, x, t)

    def to_x(dst_of, sem, rsem):
        @pl.loop(1, XS)
        def _(k):
            t = lax.rem(x + k, XS)
            s_ref, d_ref = dst_of(t)
            send(s_ref, d_ref, sem, rsem.at[x], r, t, z)

    def to_r(dst_of, sem, rsem):
        @pl.loop(1, ROWS)
        def _(k):
            t = lax.rem(r + k, ROWS)
            s_ref, d_ref = dst_of(t)
            send(s_ref, d_ref, sem, rsem.at[r], t, x, z)

    def with_own(first, rest, src, dst, ssem0, rsem):
        @pl.when(diagonal)
        def _():
            pltpu.make_async_copy(src, dst, rsem).start()

        @pl.when(jnp.logical_not(diagonal))
        def _():
            send(src, dst, ssem0, rsem, *first)

        rest()

    def to_cross(src_of, dst, ssem, ssem0, rsem):
        def rest():
            @pl.loop(1, ZS)
            def _(k):
                t = lax.rem(z + k, ZS)
                send(src_of(t), dst, ssem, rsem.at[r], z, x, t)

        with_own((z, x, z), rest, src_of(z), dst, ssem0, rsem.at[r])

    def part_rows(j):
        return pl.ds(pl.multiple_of(j * PART, 8), PART)

    def small_rows(j):
        return pl.ds(pl.multiple_of(j * GP, 8), GP)

    def split_columns(source):
        high, low = halves(source[...])
        chl[:, :K] = high
        chl[:, K:] = low

    def products_by_rows(m):
        for b in range(NBC):
            depth = (b + 1) * BS
            right = chl[:depth, :]
            both = jnp.dot(ahi[b, :, :depth], right, preferred_element_type=F32) + jnp.dot(
                alo[b, :, :depth], right, preferred_element_type=F32
            )
            total = both[:, :K] + both[:, K:]
            for xx in range(XS):
                p[m, xx, b * BS : (b + 1) * BS, :] = total[xx * BS : (xx + 1) * BS, :]

    def turn_rows(source):
        for b in range(NBC):

            @pl.loop(0, XS)
            def _(xx):
                high, low = halves(source[xx, b * BS : (b + 1) * BS, :].T)
                at = pl.ds(pl.multiple_of(xx * BS, BS), BS)
                rt[b, :K, at] = high
                rt[b, K:, at] = low

    def products_by_columns(m):
        for b in reversed(range(NBC)):
            depth = (b + 1) * BS
            left = rt[b]
            both = jnp.dot(left, ahi[b, :, :depth], preferred_element_type=F32) + jnp.dot(
                left, alo[b, :, :depth], preferred_element_type=F32
            )
            total = both[:K, :] + both[K:, :]
            if b == NBC - 1:
                yt[...] = total
            else:
                yt[:, :depth] += total
        for b in range(NBC):
            yv[m, b * BS : (b + 1) * BS, :] = yt[:, b * BS : (b + 1) * BS].T

    def gram_rows(left, right):
        def step(xx, total):
            return total + dot_t(left[xx], right[xx])

        return lax.fori_loop(0, XS, step, jnp.zeros((K, K), F32))

    lanes = lax.broadcasted_iota(jnp.int32, (K, K), 1)
    subs = lax.broadcasted_iota(jnp.int32, (K, K), 0)
    lane_row = lax.broadcasted_iota(jnp.int32, (1, K), 1)

    def eliminate(now, rows, first):
        hits = [lane_row == first + a for a in range(FOUR)]
        any_hit = hits[0] | hits[1] | hits[2] | hits[3]
        cols = [
            jnp.sum(jnp.where(lanes == first + a, now, 0.0), axis=1, keepdims=True)
            for a in range(FOUR)
        ]
        block = [
            [jnp.sum(jnp.where(h, row, 0.0), axis=1, keepdims=True) for h in hits] for row in rows
        ]
        rows = [
            jnp.where(any_hit, jnp.where(h, 1.0, 0.0), row) for h, row in zip(hits, rows)
        ]
        scale = []
        for a in range(FOUR):
            scale.append(1.0 / block[a][a])
            for b in range(a + 1, FOUR):
                factor = block[b][a] * scale[a]
                for c in range(a + 1, FOUR):
                    block[b][c] = block[b][c] - factor * block[a][c]
                rows[b] = rows[b] - factor * rows[a]
        for a in reversed(range(FOUR)):
            for b in range(a + 1, FOUR):
                rows[a] = rows[a] - block[a][b] * rows[b]
            rows[a] = rows[a] * scale[a]
        now = jnp.where((lanes >= first) & (lanes < first + FOUR), 0.0, now)
        for a in range(FOUR):
            now = now - cols[a] * rows[a]
        for a in range(FOUR):
            now = jnp.where(subs == first + a, rows[a], now)
        return now

    def pivots(slots, first, last):
        @pl.loop(first // FOUR, last // FOUR)
        def _(i):
            done = [
                eliminate(mat[s], [mat[s, pl.ds(FOUR * i + a, 1), :] for a in range(FOUR)], FOUR * i)
                for s in slots
            ]
            for s, value in zip(slots, done):
                mat[s] = value

    def sum_start(k, value, sem):
        gsrc[k] = value
        to_r(lambda t: (gsrc.at[k, small_rows(t)], grs.at[k, r]), sem, grs_sem.at[k])

    def sum_middle(k):
        grs[k, r] = gsrc[k, small_rows(r)]

        @pl.loop(1, ROWS)
        def _(j):
            t = lax.rem(r + j, ROWS)
            await_bytes(grs.at[k, t], grs_sem.at[k, t])

        total = grs[k, 0]
        for j in range(1, ROWS):
            total = total + grs[k, j]
        return total

    def sum_spread(k, total, sem):
        gfull[k, small_rows(r)] = total
        piece = gfull.at[k, small_rows(r)]
        to_r(lambda t: (piece, piece), sem, gag_sem.at[k])

    def sum_end(k):
        @pl.loop(1, ROWS)
        def _(j):
            t = lax.rem(r + j, ROWS)
            await_bytes(gfull.at[k, small_rows(t)], gag_sem.at[k, t])

        return gfull[k]

    def wide_z(k):
        gz[k, z] = sum_middle(k)
        to_z(lambda t: (gz.at[k, z], gz.at[k, z]), snd.at[WIDE + 2 * k], gz_sem.at[k])

    def wide_x(k):
        @pl.loop(1, ZS)
        def _(j):
            t = lax.rem(z + j, ZS)
            await_bytes(gz.at[k, t], gz_sem.at[k, t])

        total = gz[k, 0]
        for j in range(1, ZS):
            total = total + gz[k, j]
        gx[k, x] = total
        to_x(lambda t: (gx.at[k, x], gx.at[k, x]), snd.at[WIDE + 1 + 2 * k], gx_sem.at[k])

    def wide_r(k, sem):
        @pl.loop(1, XS)
        def _(j):
            t = lax.rem(x + j, XS)
            await_bytes(gx.at[k, t], gx_sem.at[k, t])

        sum_spread(k, (gx[k, 0] + gx[k, 1]) + (gx[k, 2] + gx[k, 3]), sem)

    split_columns(cb)

    mine = x * ZS + z
    for b in range(NBC):
        load_a(b).wait()

        @pl.loop(0, XS)
        def _(xx):
            there = xx * ZS + r
            weight = jnp.where(there > mine, 1.0, jnp.where(there == mine, 0.5, 0.0)).astype(F32)
            at = pl.ds(pl.multiple_of(xx * BS, BS), BS)
            for bb in range(b + 1):
                block = araw[pl.ds((b * XS + xx) * SET + bb, BS, NBC), :]
                if bb == b:
                    block = block * weight
                high, low = halves(block)
                ahi[b, at, bb * BS : (bb + 1) * BS] = high
                alo[b, at, bb * BS : (bb + 1) * BS] = low

    def scatter_rows(m, first, last):
        @pl.loop(first, last)
        def _(k):
            at = part_rows(lax.rem(z + k, ZS))
            sem = x_sem.at[m, x, lax.rem(z + k, ZS)]
            for far in (1, 3, 2):
                t = lax.rem(x + far, XS)
                send(p.at[m, t, at], rx.at[m, x, at], snd.at[1 + m], sem, r, t, z)

    def sum_x(m, slot):
        at = part_rows(slot)
        total = p[m, x, at]
        for far in (1, 3, 2):
            t = lax.rem(x + far, XS)
            await_bytes(rx.at[m, t, at], x_sem.at[m, t, slot])
            total = total + rx[m, t, at]
        return total

    def scatter_rows_next(m, first, last):
        @pl.loop(first, last)
        def _(k):
            slot = lax.rem(z + k, ZS)
            q[m, part_rows(slot)] = sum_x(m, slot)
            send(
                q.at[m, part_rows(slot)], rz.at[m, z], snd.at[3 + m], z_sem.at[m, z], r, x, slot
            )

    def scatter_columns(m):
        to_r(
            lambda t: (yv.at[m, part_rows(t)], ry.at[m, r]), snd.at[5 + m], y_sem.at[m]
        )

    def columns_sum(m):
        ry[m, r] = yv[m, part_rows(r)]

        @pl.loop(1, ROWS)
        def _(k):
            t = lax.rem(r + k, ROWS)
            await_bytes(ry.at[m, t], y_sem.at[m, t])

        total = ry[m, 0]
        for j in range(1, ROWS):
            total = total + ry[m, j]
        ysum[m] = total

        @pl.when(diagonal)
        def _():
            ycross[m] = ysum[m]

        @pl.when(jnp.logical_not(diagonal))
        def _():
            send(ysum.at[m], ycross.at[m], snd0.at[1 + m], yx_sem.at[m], z, x, r)

    def owned(m):
        rz[m, z] = sum_x(m, z)

        @pl.when(jnp.logical_not(diagonal))
        def _():
            await_bytes(ycross.at[m], yx_sem.at[m])

        @pl.loop(1, ZS)
        def _(k):
            t = lax.rem(z + k, ZS)
            await_bytes(rz.at[m, t], z_sem.at[m, t])

        total = rz[m, 0] + ycross[m]
        for j in range(1, 8):
            total = total + rz[m, j]
        own[m] = total

    def swap_start(m):
        @pl.when(diagonal)
        def _():
            swapped[m] = own[m]

        @pl.when(jnp.logical_not(diagonal))
        def _():
            send(own.at[m], swapped.at[m], snd0.at[3 + m], w_sem.at[m], z, x, r)

    def swap_spread(m, dst):
        @pl.when(jnp.logical_not(diagonal))
        def _():
            await_bytes(swapped.at[m], w_sem.at[m])

        dst[part_rows(r)] = swapped[m]
        piece = dst.at[part_rows(r)]
        to_r(lambda t: (piece, piece), snd.at[7 + m], c_sem.at[m])

    def columns_here(m, dst):
        @pl.loop(1, ROWS)
        def _(k):
            t = lax.rem(r + k, ROWS)
            await_bytes(dst.at[part_rows(t)], c_sem.at[m, t])

    def forward(rows, slot, ssem, rsem):
        piece = rows.at[x, part_rows(slot)]
        for far in (1, 3, 2):
            send(piece, piece, ssem, rsem.at[x], r, lax.rem(x + far, XS), z)

    def rows_here(rows, rsem):
        @pl.loop(1, XS)
        def _(k):
            t = lax.rem(x + k, XS)
            await_bytes(rows.at[t], rsem.at[t])

    products_by_rows(0)

    @pl.when(jnp.logical_not(diagonal))
    def _():
        pl.semaphore_wait(barrier, 25)

    @pl.when(diagonal)
    def _():
        pl.semaphore_wait(barrier, 24)

    to_cross(
        lambda t: cb.at[part_rows(r)], rb.at[x, part_rows(r)], snd.at[0], snd0.at[0], rb_z
    )
    scatter_rows(0, 1, 3)

    @pl.loop(0, ROWS)
    def _(k):
        slot = lax.rem(r + k, ROWS)
        await_bytes(rb.at[x, part_rows(slot)], rb_z.at[slot])
        forward(rb, slot, snd.at[9], rb_x)

    rows_here(rb, rb_x)
    scatter_rows(0, 3, ZS + 1)
    turn_rows(rb)
    products_by_columns(0)
    scatter_columns(0)
    sum_start(1, gram_rows(rb, p.at[0]), snd.at[14])
    scatter_rows_next(0, 1, 3)
    columns_sum(0)
    scatter_rows_next(0, 3, 5)
    wide_z(1)
    scatter_rows_next(0, 5, 8)
    sum_start(0, gram_rows(rb, rb), snd.at[10])
    wide_x(1)
    owned(0)

    swap_start(0)
    rw[x, part_rows(z)] = own[0]
    to_z(lambda t: (own.at[0], rw.at[x, part_rows(z)]), snd.at[12], rw_z)
    forward(rw, z, snd.at[13], rw_x)
    sum_spread(0, sum_middle(0), snd.at[11])
    wide_r(1, snd.at[15])

    def onward(k):
        slot = lax.rem(z + k, ZS)
        await_bytes(rw.at[x, part_rows(slot)], rw_z.at[slot])
        forward(rw, slot, snd.at[13], rw_x)

    chunk = K // 4
    for k, far in enumerate((1, 7, 2, 6, 3, 5, 4)):
        onward(far)
        if k == 1:
            mat[0] = sum_end(0)
        if k in (1, 2):
            pivots((0,), (k - 1) * K // 2, k * K // 2)
        if k == 3:
            swap_spread(0, cw)
            half = sum_end(1)
            mat[1] = half + half.T
        if k > 3:
            pivots((1,), (k - 4) * chunk, (k - 3) * chunk)
    columns_here(0, cw)
    split_columns(cw)
    products_by_rows(1)
    scatter_rows(1, 1, ZS + 1)
    pivots((1,), K - chunk, K)
    step = dot(mat[1], gfull[0])
    rows_here(rw, rw_x)
    turn_rows(rw)
    products_by_columns(1)
    scatter_columns(1)
    scatter_rows_next(1, 1, 3)

    def residual_gram(xx, total):
        part = rb[xx] - dot(rw[xx], step)
        return total + dot_t(part, part)

    sum_start(2, lax.fori_loop(0, XS, residual_gram, jnp.zeros((K, K), F32)), snd.at[16])
    columns_sum(1)
    scatter_rows_next(1, 3, 6)
    sum_spread(2, sum_middle(2), snd.at[17])
    scatter_rows_next(1, 6, 8)
    owned(1)
    swap_start(1)
    mix = dot(mat[0], sum_end(2))
    b_own = rb[x, part_rows(z)]
    r_own = b_own - dot(own[0], step)

    def image_of(wide, wider):
        return wide + dot(wide, mix) - dot(wider, step)

    d_own = r_own + dot(b_own, mix)
    sum_start(3, dot_t(d_own, image_of(own[0], own[1])), snd.at[18])
    res = cb[...] - dot(cw[...], step)
    cres[...] = res
    cdir[...] = res + dot(cb[...], mix)
    wide_z(3)
    swap_spread(1, cv)
    wide_x(3)
    out_x[...] = dot(cb[...], step)
    wide_r(3, snd.at[19])
    columns_here(1, cv)
    cimg[...] = image_of(cw[...], cv[...])
    mat[0] = sum_end(3)
    pivots((0,), 0, K)
    step2 = dot(mat[0], gfull[2])
    out_x[...] += dot(cdir[...], step2)
    out_r[...] = cres[...] - dot(cimg[...], step2)

    small = 7 * GP
    wide = tuple((WIDE + 2 * k + j, rows) for k in (1, 3) for j, rows in ((0, small), (1, 3 * GP)))
    for index, rows in wide + (
        (0, 7 * PART), (1, 3 * SET), (2, 3 * SET), (3, 7 * PART), (4, 7 * PART),
        (5, 7 * PART), (6, 7 * PART), (7, 7 * PART), (8, 7 * PART), (9, 3 * SET),
        (10, small), (11, small), (12, 7 * PART), (13, 3 * SET), (14, small), (15, small),
        (16, small), (17, small), (18, small), (19, small),
    ):
        await_sent(snd.at[index], rows)

    @pl.when(jnp.logical_not(diagonal))
    def _():
        for index in range(5):
            await_sent(snd0.at[index], PART)


def per_device(stored, rhs):
    vm = pltpu.VMEM
    dma = pltpu.SemaphoreType.DMA
    outs = pl.pallas_call(
        kernel,
        out_shape=(jax.ShapeDtypeStruct((SET, K), F32), jax.ShapeDtypeStruct((SET, K), F32)),
        in_specs=[pl.BlockSpec(memory_space=pl.ANY), pl.BlockSpec(memory_space=pl.ANY)],
        out_specs=(pl.BlockSpec(memory_space=pltpu.VMEM), pl.BlockSpec(memory_space=pltpu.VMEM)),
        scratch_shapes=[
            vm((NBC * XS * SET, BS), F32),
            vm((NBC, XS * BS, SET), BF16),
            vm((NBC, XS * BS, SET), BF16),
            vm((SET, K), F32),
            vm((SET, K), F32),
            vm((SET, K), F32),
            vm((SET, 2 * K), BF16),
            vm((XS, SET, K), F32),
            vm((XS, SET, K), F32),
            vm((NBC, 2 * K, XS * BS), BF16),
            vm((K, SET), F32),
            vm((2, XS, SET, K), F32),
            vm((2, XS, SET, K), F32),
            vm((2, SET, K), F32),
            vm((2, ZS, PART, K), F32),
            vm((2, SET, K), F32),
            vm((2, ROWS, PART, K), F32),
            vm((2, PART, K), F32),
            vm((2, PART, K), F32),
            vm((2, PART, K), F32),
            vm((2, PART, K), F32),
            vm((4, K, K), F32),
            vm((4, ROWS, GP, K), F32),
            vm((4, K, K), F32),
            vm((4, ZS, GP, K), F32),
            vm((4, XS, GP, K), F32),
            vm((2, K, K), F32),
            vm((SET, K), F32),
            vm((SET, K), F32),
            vm((SET, K), F32),
            dma((NBC + 1,)),
            dma((28,)),
            dma((5,)),
            dma((ROWS,)),
            dma((XS,)),
            dma((2, XS, ZS)),
            dma((2, ZS)),
            dma((2, ROWS)),
            dma((2, ROWS)),
            dma((2,)),
            dma((2,)),
            dma((ZS,)),
            dma((XS,)),
            dma((4, ROWS)),
            dma((4, ROWS)),
            dma((4, ZS)),
            dma((4, XS)),
        ],
        compiler_params=pltpu.CompilerParams(
            collective_id=0, has_side_effects=True, vmem_limit_bytes=56 * 2**20
        ),
        name="block_cg",
    )(stored.reshape(-1, BS), rhs.reshape(-1, K))
    return tuple(o.reshape(rhs.shape) for o in outs)


def solution(mesh):
    return jax.shard_map(
        per_device,
        mesh=mesh,
        in_specs=(P(None, "row", None, None, "col", None), P(None, "col", None, None)),
        out_specs=(P(None, "col", None, None), P(None, "col", None, None)),
        check_vma=False,
    )
```

```python
import functools

import jax
import jax.numpy as jnp
from jax import lax
from jax.experimental import pallas as pl
from jax.experimental.pallas import tpu as pltpu
from jax.sharding import PartitionSpec as P

MESH = pl.DeviceIdType.MESH
HIGHEST = lax.Precision.HIGHEST
F32 = jnp.float32
BF16 = jnp.bfloat16

ROWS = 8
XS = 4
ZS = 8
NBC = 5
BS = 128
K = 128
SET = NBC * BS
PART = SET // ROWS
GP = K // ROWS
FOUR = 4
WIDE = 20


def dot(a, b):
    return jnp.dot(a, b, precision=HIGHEST, preferred_element_type=F32)


def dot_t(a, b):
    return lax.dot_general(
        a, b, (((0,), (0,)), ((), ())), precision=HIGHEST, preferred_element_type=F32
    )


def halves(value):
    high = value.astype(BF16)
    low = (value - high.astype(F32)).astype(BF16)
    return high, low


def kernel(
    stored, rhs, out_x, out_r,
    araw, ahi, alo, cb, cw, cv, chl, rb, rw, rt, yt,
    p, rx, q, rz, yv, ry, own, swapped,
    gsrc, grs, gfull, gz, gx, mat, cres, cdir, cimg,
    ld_sem, snd, snd0, rb_z, rb_x, x_sem, z_sem, y_sem, c_sem, w_sem, rw_z, rw_x,
    grs_sem, gag_sem, gz_sem, gx_sem,
):
    r = lax.axis_index("row")
    c = lax.axis_index("col")
    x = c // ZS
    z = lax.rem(c, ZS)
    diagonal = r == z

    def send(src, dst, ssem, rsem, row, xx, zz):
        pltpu.make_async_remote_copy(
            src_ref=src, dst_ref=dst, send_sem=ssem, recv_sem=rsem,
            device_id=(row, xx * ZS + zz), device_id_type=MESH,
        ).start()

    def await_bytes(ref, sem):
        pltpu.make_async_copy(ref, ref, sem).wait()

    def await_sent(sem, rows):
        part = araw.at[pl.ds(0, rows)]
        pltpu.make_async_copy(part, part, sem).wait()

    load_b = pltpu.make_async_copy(rhs, cb, ld_sem.at[NBC])
    load_b.start()
    span = XS * SET

    def load_a(b):
        rows = pl.ds(b * span, span)
        return pltpu.make_async_copy(stored.at[rows], araw.at[rows], ld_sem.at[b])

    for b in range(NBC):
        load_a(b).start()

    barrier = pltpu.get_barrier_semaphore()

    def greet(row, xx, zz):
        pl.semaphore_signal(barrier, inc=1, device_id=(row, xx * ZS + zz), device_id_type=MESH)

    @pl.loop(1, 8)
    def _(k):
        greet(r, x, lax.rem(z + k, ZS))
        greet(lax.rem(r + k, ROWS), x, z)
        greet(lax.rem(r + k, ROWS), x, r)

    @pl.loop(1, XS)
    def _(k):
        greet(r, lax.rem(x + k, XS), z)

    @pl.when(jnp.logical_not(diagonal))
    def _():
        greet(r, x, r)

    load_b.wait()

    def to_z(dst_of, sem, rsem):

        @pl.loop(1, ZS)
        def _(k):
            t = lax.rem(z + k, ZS)
            s_ref, d_ref = dst_of(t)
            send(s_ref, d_ref, sem, rsem.at[z], r, x, t)

    def to_x(dst_of, sem, rsem):
        @pl.loop(1, XS)
        def _(k):
            t = lax.rem(x + k, XS)
            s_ref, d_ref = dst_of(t)
            send(s_ref, d_ref, sem, rsem.at[x], r, t, z)

    def to_r(dst_of, sem, rsem):
        @pl.loop(1, ROWS)
        def _(k):
            t = lax.rem(r + k, ROWS)
            s_ref, d_ref = dst_of(t)
            send(s_ref, d_ref, sem, rsem.at[r], t, x, z)

    def with_own(first, rest, src, dst, ssem0, rsem):
        @pl.when(diagonal)
        def _():
            pltpu.make_async_copy(src, dst, rsem).start()

        @pl.when(jnp.logical_not(diagonal))
        def _():
            send(src, dst, ssem0, rsem, *first)

        rest()

    def to_cross(src_of, dst, ssem, ssem0, rsem):
        def rest():
            @pl.loop(1, ZS)
            def _(k):
                t = lax.rem(z + k, ZS)
                send(src_of(t), dst, ssem, rsem.at[r], z, x, t)

        with_own((z, x, z), rest, src_of(z), dst, ssem0, rsem.at[r])

    def part_rows(j):
        return pl.ds(pl.multiple_of(j * PART, 8), PART)

    def small_rows(j):
        return pl.ds(pl.multiple_of(j * GP, 8), GP)

    def split_columns(source):
        high, low = halves(source[...])
        chl[:, :K] = high
        chl[:, K:] = low

    def products_by_rows(m):
        for b in range(NBC):
            depth = (b + 1) * BS
            right = chl[:depth, :]
            both = jnp.dot(ahi[b, :, :depth], right, preferred_element_type=F32) + jnp.dot(
                alo[b, :, :depth], right, preferred_element_type=F32
            )
            total = both[:, :K] + both[:, K:]
            for xx in range(XS):
                p[m, xx, b * BS : (b + 1) * BS, :] = total[xx * BS : (xx + 1) * BS, :]

    def turn_rows(source):
        for b in range(NBC):

            @pl.loop(0, XS)
            def _(xx):
                high, low = halves(source[xx, b * BS : (b + 1) * BS, :].T)
                at = pl.ds(pl.multiple_of(xx * BS, BS), BS)
                rt[b, :K, at] = high
                rt[b, K:, at] = low

    def products_by_columns(m):
        for b in reversed(range(NBC)):
            depth = (b + 1) * BS
            left = rt[b]
            both = jnp.dot(left, ahi[b, :, :depth], preferred_element_type=F32) + jnp.dot(
                left, alo[b, :, :depth], preferred_element_type=F32
            )
            total = both[:K, :] + both[K:, :]
            if b == NBC - 1:
                yt[...] = total
            else:
                yt[:, :depth] += total
        for b in range(NBC):
            yv[m, b * BS : (b + 1) * BS, :] = yt[:, b * BS : (b + 1) * BS].T

    def gram_rows(left, right):
        def step(xx, total):
            return total + dot_t(left[xx], right[xx])

        return lax.fori_loop(0, XS, step, jnp.zeros((K, K), F32))

    lanes = lax.broadcasted_iota(jnp.int32, (K, K), 1)
    subs = lax.broadcasted_iota(jnp.int32, (K, K), 0)
    lane_row = lax.broadcasted_iota(jnp.int32, (1, K), 1)

    def eliminate(now, rows, first):
        hits = [lane_row == first + a for a in range(FOUR)]
        any_hit = hits[0] | hits[1] | hits[2] | hits[3]
        cols = [
            jnp.sum(jnp.where(lanes == first + a, now, 0.0), axis=1, keepdims=True)
            for a in range(FOUR)
        ]
        block = [
            [jnp.sum(jnp.where(h, row, 0.0), axis=1, keepdims=True) for h in hits] for row in rows
        ]
        rows = [
            jnp.where(any_hit, jnp.where(h, 1.0, 0.0), row) for h, row in zip(hits, rows)
        ]
        scale = []
        for a in range(FOUR):
            scale.append(1.0 / block[a][a])
            for b in range(a + 1, FOUR):
                factor = block[b][a] * scale[a]
                for c in range(a + 1, FOUR):
                    block[b][c] = block[b][c] - factor * block[a][c]
                rows[b] = rows[b] - factor * rows[a]
        for a in reversed(range(FOUR)):
            for b in range(a + 1, FOUR):
                rows[a] = rows[a] - block[a][b] * rows[b]
            rows[a] = rows[a] * scale[a]
        now = jnp.where((lanes >= first) & (lanes < first + FOUR), 0.0, now)
        for a in range(FOUR):
            now = now - cols[a] * rows[a]
        for a in range(FOUR):
            now = jnp.where(subs == first + a, rows[a], now)
        return now

    def pivots(slots, first, last):
        @pl.loop(first // FOUR, last // FOUR)
        def _(i):
            done = [
                eliminate(mat[s], [mat[s, pl.ds(FOUR * i + a, 1), :] for a in range(FOUR)], FOUR * i)
                for s in slots
            ]
            for s, value in zip(slots, done):
                mat[s] = value

    def sum_start(k, value, sem):
        gsrc[k] = value
        to_r(lambda t: (gsrc.at[k, small_rows(t)], grs.at[k, r]), sem, grs_sem.at[k])

    def sum_middle(k):
        grs[k, r] = gsrc[k, small_rows(r)]

        @pl.loop(1, ROWS)
        def _(j):
            t = lax.rem(r + j, ROWS)
            await_bytes(grs.at[k, t], grs_sem.at[k, t])

        total = grs[k, 0]
        for j in range(1, ROWS):
            total = total + grs[k, j]
        return total

    def sum_spread(k, total, sem):
        gfull[k, small_rows(r)] = total
        piece = gfull.at[k, small_rows(r)]
        to_r(lambda t: (piece, piece), sem, gag_sem.at[k])

    def sum_end(k):
        @pl.loop(1, ROWS)
        def _(j):
            t = lax.rem(r + j, ROWS)
            await_bytes(gfull.at[k, small_rows(t)], gag_sem.at[k, t])

        return gfull[k]

    def wide_z(k):
        gz[k, z] = sum_middle(k)
        to_z(lambda t: (gz.at[k, z], gz.at[k, z]), snd.at[WIDE + 2 * k], gz_sem.at[k])

    def wide_x(k):
        @pl.loop(1, ZS)
        def _(j):
            t = lax.rem(z + j, ZS)
            await_bytes(gz.at[k, t], gz_sem.at[k, t])

        total = gz[k, 0]
        for j in range(1, ZS):
            total = total + gz[k, j]
        gx[k, x] = total
        to_x(lambda t: (gx.at[k, x], gx.at[k, x]), snd.at[WIDE + 1 + 2 * k], gx_sem.at[k])

    def wide_r(k, sem):
        @pl.loop(1, XS)
        def _(j):
            t = lax.rem(x + j, XS)
            await_bytes(gx.at[k, t], gx_sem.at[k, t])

        sum_spread(k, (gx[k, 0] + gx[k, 1]) + (gx[k, 2] + gx[k, 3]), sem)

    split_columns(cb)

    mine = x * ZS + z
    for b in range(NBC):
        load_a(b).wait()

        @pl.loop(0, XS)
        def _(xx):
            there = xx * ZS + r
            weight = jnp.where(there > mine, 1.0, jnp.where(there == mine, 0.5, 0.0)).astype(F32)
            at = pl.ds(pl.multiple_of(xx * BS, BS), BS)
            for bb in range(b + 1):
                block = araw[pl.ds((b * XS + xx) * SET + bb, BS, NBC), :]
                if bb == b:
                    block = block * weight
                high, low = halves(block)
                ahi[b, at, bb * BS : (bb + 1) * BS] = high
                alo[b, at, bb * BS : (bb + 1) * BS] = low

    def scatter_rows(m, first, last):
        @pl.loop(first, last)
        def _(k):
            at = part_rows(lax.rem(z + k, ZS))
            sem = x_sem.at[m, x, lax.rem(z + k, ZS)]
            for far in (1, 3, 2):
                t = lax.rem(x + far, XS)
                send(p.at[m, t, at], rx.at[m, x, at], snd.at[1 + m], sem, r, t, z)

    def sum_x(m, slot):
        at = part_rows(slot)
        total = p[m, x, at]
        for far in (1, 3, 2):
            t = lax.rem(x + far, XS)
            await_bytes(rx.at[m, t, at], x_sem.at[m, t, slot])
            total = total + rx[m, t, at]
        return total

    def scatter_rows_next(m, first, last):
        @pl.loop(first, last)
        def _(k):
            slot = lax.rem(z + k, ZS)
            q[m, part_rows(slot)] = sum_x(m, slot)
            send(
                q.at[m, part_rows(slot)], rz.at[m, z], snd.at[3 + m], z_sem.at[m, z], r, x, slot
            )

    def scatter_columns(m):
        to_cross(
            lambda t: yv.at[m, part_rows(t)], ry.at[m, r], snd.at[5 + m], snd0.at[1 + m], y_sem.at[m]
        )

    def owned(m):
        rz[m, z] = sum_x(m, z)

        @pl.loop(1, ZS)
        def _(k):
            t = lax.rem(z + k, ZS)
            await_bytes(rz.at[m, t], z_sem.at[m, t])

        @pl.loop(0, ROWS)
        def _(k):
            await_bytes(ry.at[m, k], y_sem.at[m, k])

        total = rz[m, 0] + ry[m, 0]
        for j in range(1, 8):
            total = total + (rz[m, j] + ry[m, j])
        own[m] = total

    def swap_start(m):
        @pl.when(diagonal)
        def _():
            swapped[m] = own[m]

        @pl.when(jnp.logical_not(diagonal))
        def _():
            send(own.at[m], swapped.at[m], snd0.at[3 + m], w_sem.at[m], z, x, r)

    def swap_spread(m, dst):
        @pl.when(jnp.logical_not(diagonal))
        def _():
            await_bytes(swapped.at[m], w_sem.at[m])

        dst[part_rows(r)] = swapped[m]
        piece = dst.at[part_rows(r)]
        to_r(lambda t: (piece, piece), snd.at[7 + m], c_sem.at[m])

    def columns_here(m, dst):
        @pl.loop(1, ROWS)
        def _(k):
            t = lax.rem(r + k, ROWS)
            await_bytes(dst.at[part_rows(t)], c_sem.at[m, t])

    def forward(rows, slot, ssem, rsem):
        piece = rows.at[x, part_rows(slot)]
        for far in (1, 3, 2):
            send(piece, piece, ssem, rsem.at[x], r, lax.rem(x + far, XS), z)

    def rows_here(rows, rsem):
        @pl.loop(1, XS)
        def _(k):
            t = lax.rem(x + k, XS)
            await_bytes(rows.at[t], rsem.at[t])

    products_by_rows(0)

    @pl.when(jnp.logical_not(diagonal))
    def _():
        pl.semaphore_wait(barrier, 25)

    @pl.when(diagonal)
    def _():
        pl.semaphore_wait(barrier, 24)

    to_cross(
        lambda t: cb.at[part_rows(r)], rb.at[x, part_rows(r)], snd.at[0], snd0.at[0], rb_z
    )
    scatter_rows(0, 1, 3)

    @pl.loop(0, ROWS)
    def _(k):
        slot = lax.rem(r + k, ROWS)
        await_bytes(rb.at[x, part_rows(slot)], rb_z.at[slot])
        forward(rb, slot, snd.at[9], rb_x)

    rows_here(rb, rb_x)
    scatter_rows(0, 3, ZS + 1)
    turn_rows(rb)
    products_by_columns(0)
    scatter_columns(0)
    sum_start(1, gram_rows(rb, p.at[0]), snd.at[14])
    sum_start(0, gram_rows(rb, rb), snd.at[10])
    scatter_rows_next(0, 1, 4)
    wide_z(1)
    sum_spread(0, sum_middle(0), snd.at[11])
    scatter_rows_next(0, 4, 8)
    mat[0] = sum_end(0)
    wide_x(1)
    owned(0)

    swap_start(0)
    rw[x, part_rows(z)] = own[0]
    to_z(lambda t: (own.at[0], rw.at[x, part_rows(z)]), snd.at[12], rw_z)
    forward(rw, z, snd.at[13], rw_x)
    wide_r(1, snd.at[15])

    def onward(k):
        slot = lax.rem(z + k, ZS)
        await_bytes(rw.at[x, part_rows(slot)], rw_z.at[slot])
        forward(rw, slot, snd.at[13], rw_x)

    chunk = K // 4
    for k, far in enumerate((1, 7, 2, 6, 3, 5, 4)):
        onward(far)
        if k == 3:
            swap_spread(0, cw)
            half = sum_end(1)
            mat[1] = half + half.T
        part = k % 4 * chunk
        pivots((k // 4,), part, part + chunk)
    columns_here(0, cw)
    split_columns(cw)
    products_by_rows(1)
    scatter_rows(1, 1, ZS + 1)
    pivots((1,), K - chunk, K)
    step = dot(mat[1], gfull[0])
    rows_here(rw, rw_x)
    turn_rows(rw)
    products_by_columns(1)
    scatter_columns(1)
    scatter_rows_next(1, 1, 3)

    def residual_gram(xx, total):
        part = rb[xx] - dot(rw[xx], step)
        return total + dot_t(part, part)

    sum_start(2, lax.fori_loop(0, XS, residual_gram, jnp.zeros((K, K), F32)), snd.at[16])
    scatter_rows_next(1, 3, 6)
    sum_spread(2, sum_middle(2), snd.at[17])
    scatter_rows_next(1, 6, 8)
    owned(1)
    swap_start(1)
    mix = dot(mat[0], sum_end(2))
    b_own = rb[x, part_rows(z)]
    r_own = b_own - dot(own[0], step)

    def image_of(wide, wider):
        return wide + dot(wide, mix) - dot(wider, step)

    d_own = r_own + dot(b_own, mix)
    sum_start(3, dot_t(d_own, image_of(own[0], own[1])), snd.at[18])
    res = cb[...] - dot(cw[...], step)
    cres[...] = res
    cdir[...] = res + dot(cb[...], mix)
    wide_z(3)
    swap_spread(1, cv)
    wide_x(3)
    out_x[...] = dot(cb[...], step)
    wide_r(3, snd.at[19])
    columns_here(1, cv)
    cimg[...] = image_of(cw[...], cv[...])
    mat[0] = sum_end(3)
    pivots((0,), 0, K)
    step2 = dot(mat[0], gfull[2])
    out_x[...] += dot(cdir[...], step2)
    out_r[...] = cres[...] - dot(cimg[...], step2)

    small = 7 * GP
    wide = tuple((WIDE + 2 * k + j, rows) for k in (1, 3) for j, rows in ((0, small), (1, 3 * GP)))
    for index, rows in wide + (
        (0, 7 * PART), (1, 3 * SET), (2, 3 * SET), (3, 7 * PART), (4, 7 * PART),
        (5, 7 * PART), (6, 7 * PART), (7, 7 * PART), (8, 7 * PART), (9, 3 * SET),
        (10, small), (11, small), (12, 7 * PART), (13, 3 * SET), (14, small), (15, small),
        (16, small), (17, small), (18, small), (19, small),
    ):
        await_sent(snd.at[index], rows)

    @pl.when(jnp.logical_not(diagonal))
    def _():
        for index in range(5):
            await_sent(snd0.at[index], PART)


def per_device(stored, rhs):
    vm = pltpu.VMEM
    dma = pltpu.SemaphoreType.DMA
    outs = pl.pallas_call(
        kernel,
        out_shape=(jax.ShapeDtypeStruct((SET, K), F32), jax.ShapeDtypeStruct((SET, K), F32)),
        in_specs=[pl.BlockSpec(memory_space=pl.ANY), pl.BlockSpec(memory_space=pl.ANY)],
        out_specs=(pl.BlockSpec(memory_space=pltpu.VMEM), pl.BlockSpec(memory_space=pltpu.VMEM)),
        scratch_shapes=[
            vm((NBC * XS * SET, BS), F32),
            vm((NBC, XS * BS, SET), BF16),
            vm((NBC, XS * BS, SET), BF16),
            vm((SET, K), F32),
            vm((SET, K), F32),
            vm((SET, K), F32),
            vm((SET, 2 * K), BF16),
            vm((XS, SET, K), F32),
            vm((XS, SET, K), F32),
            vm((NBC, 2 * K, XS * BS), BF16),
            vm((K, SET), F32),
            vm((2, XS, SET, K), F32),
            vm((2, XS, SET, K), F32),
            vm((2, SET, K), F32),
            vm((2, ZS, PART, K), F32),
            vm((2, SET, K), F32),
            vm((2, ROWS, PART, K), F32),
            vm((2, PART, K), F32),
            vm((2, PART, K), F32),
            vm((4, K, K), F32),
            vm((4, ROWS, GP, K), F32),
            vm((4, K, K), F32),
            vm((4, ZS, GP, K), F32),
            vm((4, XS, GP, K), F32),
            vm((2, K, K), F32),
            vm((SET, K), F32),
            vm((SET, K), F32),
            vm((SET, K), F32),
            dma((NBC + 1,)),
            dma((28,)),
            dma((5,)),
            dma((ROWS,)),
            dma((XS,)),
            dma((2, XS, ZS)),
            dma((2, ZS)),
            dma((2, ROWS)),
            dma((2, ROWS)),
            dma((2,)),
            dma((ZS,)),
            dma((XS,)),
            dma((4, ROWS)),
            dma((4, ROWS)),
            dma((4, ZS)),
            dma((4, XS)),
        ],
        compiler_params=pltpu.CompilerParams(
            collective_id=0, has_side_effects=True, vmem_limit_bytes=56 * 2**20
        ),
        name="block_cg",
    )(stored.reshape(-1, BS), rhs.reshape(-1, K))
    return tuple(o.reshape(rhs.shape) for o in outs)


def solution(mesh):
    return jax.shard_map(
        per_device,
        mesh=mesh,
        in_specs=(P(None, "row", None, None, "col", None), P(None, "col", None, None)),
        out_specs=(P(None, "col", None, None), P(None, "col", None, None)),
        check_vma=False,
    )
```
